256 devices in a mesh: dp: 8 (over x_lo, y), owner: 8 (over z), context: 4 (over x_hi, core).
Axes of the slice: x: 4 (x_hi: 2, x_lo: 2; x = x_hi * 2 + x_lo), y: 4, z: 8, core: 2. Of those that a mesh axis runs over, the one named last changes fastest.
Arguments:
- grad_partials: bfloat16 [32, 1536, 64, 192], P(('dp', 'context'), None, 'owner')
- assignment: int32 [64, 1], replicated, may hold values from 0 to 7; in each aligned block of 8 rows (0 to 7, 8 to 15, ...) at most 2 rows name the same one
- momentum: float32 [128, 1536, 192], P('owner', ('dp', 'context')), may hold values from -6 to 6
- q_weight: float32 [128, 1536, 192], P('owner', ('dp', 'context')), may hold values from -1.2 to 1.2
- k_weight: float32 [64, 512, 128], P('owner', ('dp', 'context')), may hold values from -6 to 6
- max_logits: float32 [4, 64], P('context'), may hold values from 20 to 400
Outputs:
- momentum_out: float32 [128, 1536, 192], P('owner', ('dp', 'context'))
- q_weight_out: float32 [128, 1536, 192], P('owner', ('dp', 'context'))
- k_weight_out: float32 [64, 512, 128], P('owner', ('dp', 'context'))
The draws below stay inside these ranges and needn't reach their ends.
Inputs may be any that keep to these rules, and one draw needn't show every extreme that they name: `assignment`: in each aligned block of 8 heads no owner index is named more than 2 times, and some owner index exactly 2 times.
All inputs are finite; a program needn't handle non-finite values.
Results may differ from the reference program's by a relative error of at most 0.0007.
Values may be sent and summed in bfloat16 or wider, within the bound.
A program may use at most 128 MiB of HBM per device.

```python
import math
import jax
import jax.numpy as jnp
import numpy as np
from jax import lax

QR = 1536
QK = 192
KN = 128
KVR = 512
HEADS_OWN = 8
C_SEND = 2
ITERS = 2
HEADS = 64
SLOTS_OWN = 16
SLOTS = 128
GRAD_PARTS = 32
LOGIT_PARTS = 4
N_OWNER = 8


def draw_grad_partials(key, part):
    key_noise = jax.random.fold_in(key, 11)
    key_rows = jax.random.fold_in(key, 12)
    key_columns = jax.random.fold_in(key, 13)
    key_left = jax.random.fold_in(key, 15)
    key_right = jax.random.fold_in(key, 16)
    row_top = 10.0
    factor_weight = 0.8
    row_scale = jnp.exp(jax.random.uniform(key_rows, (1, QR, 1, 1), jnp.float32, 0.0, math.log(row_top)))
    column_scale = jnp.exp(jax.random.uniform(key_columns, (1, 1, 1, QK), jnp.float32, 0.0, math.log(10.0)))
    block_rows = QR // GRAD_PARTS
    half_blocks = max(GRAD_PARTS // 2, 1)
    row_block = jnp.arange(QR, dtype=jnp.int32) // block_rows
    pair_index = row_block % half_blocks
    head_index = jnp.arange(HEADS, dtype=jnp.int32)
    column_target = (pair_index[:, None] * 5 + head_index[None, :] * 3) % QK
    column_index = jnp.arange(QK, dtype=jnp.int32)
    marked = (column_target[:, :, None] == column_index[None, None, :]).astype(jnp.float32)[None]
    boost = 1.0 + 5.0 * marked
    left_factor = jax.random.normal(key_left, (3, QR, HEADS), jnp.float32)
    right_factor = jax.random.normal(key_right, (3, HEADS, QK), jnp.float32)
    coupled = left_factor[0][:, :, None] * right_factor[0][None, :, :]
    coupled = coupled + left_factor[1][:, :, None] * right_factor[1][None, :, :]
    coupled = coupled + left_factor[2][:, :, None] * right_factor[2][None, :, :]
    coupled = coupled[None] * (factor_weight / GRAD_PARTS)
    values = jax.random.normal(key_noise, (GRAD_PARTS, QR, HEADS, QK), jnp.float32) / math.sqrt(GRAD_PARTS)
    return ((values + coupled) * boost * row_scale * column_scale * 0.07).astype(jnp.bfloat16)


def steps_of(stream_key, shape, cuts, low, largest):
    level, own = 1.0, jax.random.fold_in(stream_key, 6)
    for axis_at, parts in cuts:
        heights = jnp.exp(jax.random.uniform(jax.random.fold_in(own, axis_at), (parts,), jnp.float32, low / len(cuts), largest / len(cuts)))
        level = level * jnp.repeat(heights, shape[axis_at] // parts).reshape([-1 if axis == axis_at else 1 for axis in range(len(shape))])
    return level


def shared_out(rng, own, number, rows, number_of, top, bound, slope):
    ranking = jax.random.permutation(rng, number_of)
    packed, common = portions_of(number_of, rows * top, bound, slope, True), portions_of(number_of, rows * top, bound, slope, False)
    places = jnp.arange(number_of)

    def named(sizes, rotation):
        used = int((sizes > 0).sum())
        fixed = max(1, used // 4)
        moved = fixed + (places - fixed + rotation * (used - fixed)) % max(1, number_of - fixed)
        return jnp.zeros((number_of,), jnp.int32).at[ranking[jnp.where(places < fixed, places, moved)]].set(jnp.asarray(sizes, jnp.int32))

    sizes = jnp.where(number % 4 == 0, named(packed, number // 4), named(common, number - number // 4 - 1))
    mixed = jax.random.permutation(jax.random.fold_in(own, 3), number_of)
    source_of, receiver = mixed[0:number_of // 2 * 2:2], mixed[1:number_of // 2 * 2:2]
    slack = jnp.minimum(sizes[source_of] - 1, bound - sizes[receiver]) // 2
    slack = jnp.where((source_of == ranking[0]) | (receiver == ranking[0]) | (sizes[receiver] == 0), 0, jnp.maximum(slack, 0))
    moved = jax.random.randint(jax.random.fold_in(own, 4), (number_of // 2,), 0, 1 << 20) % (slack + 1)
    sizes = sizes.at[source_of].add(-moved).at[receiver].add(moved)
    items = jnp.searchsorted(jnp.cumsum(sizes), jnp.arange(rows * top), side="right").astype(jnp.int32)
    table = items.reshape(top, rows).T
    table = table[jax.random.permutation(jax.random.fold_in(own, 1), rows)]
    rotation = jax.random.randint(jax.random.fold_in(own, 2), (rows, 1), 0, top)
    return jnp.take_along_axis(table, (jnp.arange(top)[None, :] + rotation) % top, axis=1)


def portions_of(amount, total, bound, slope, full):
    loads = [(1 << 20) // math.isqrt(grade ** slope) + 1 for grade in range(1, amount + 1)]
    largest = bound if full else min(bound, max(-(-total // amount), total * loads[0] // sum(loads)))
    least = 1 if total - largest >= amount - 1 else 0
    holding, spare = [largest] + [least] * (amount - 1), total - largest - least * (amount - 1)
    while spare > 0:
        candidates = [i for i in range(1, amount) if holding[i] < largest] or [i for i in range(1, amount) if holding[i] < bound]
        pool, budget = sum([loads[i] for i in candidates]), spare
        for i in candidates:
            more = min(bound - holding[i], max(1, budget * loads[i] // pool), spare)
            holding[i] = holding[i] + more
            spare = spare - more
    return np.array(holding)


def centred(stream_key, shape, width, most, split=(), kind=jnp.bfloat16):
    drawn = jax.random.normal(stream_key, shape, jnp.float32) * width
    if len(split) > 0:
        drawn = steps_of(stream_key, shape, split, -0.22, 0.18) * drawn
    return jnp.clip(drawn, min=-most, max=most).astype(kind)


def setup_inputs(seed: int = 0) -> dict:
    key_of = jax.random.split(jax.random.key(seed), 7)
    grad_partials = draw_grad_partials(jax.random.fold_in(key_of[6], 71), 0)
    assignment_keys = jax.random.split(jax.random.fold_in(key_of[1], 1), HEADS // HEADS_OWN)
    assignment_turns = jax.random.permutation(jax.random.fold_in(key_of[1], 3), HEADS // HEADS_OWN)
    assignment = jax.vmap(lambda own, number: shared_out(jax.random.fold_in(key_of[1], 2), own, number, HEADS_OWN, N_OWNER, 1, C_SEND, 2))(assignment_keys, assignment_turns).reshape((HEADS, 1))
    momentum = centred(key_of[2], (SLOTS, QR, QK), 1.0, 6.0, ((0, 8), (1, 32)), jnp.float32)
    q_weight = centred(key_of[3], (SLOTS, QR, QK), 0.2, 1.2, ((0, 8), (1, 32)), jnp.float32)
    k_weight = centred(key_of[4], (HEADS, KVR, KN), 1.0, 6.0, ((0, 8), (1, 32)), jnp.float32)
    max_logits = jnp.clip(jnp.exp(math.log(400.0) - 2.9957323 * jax.random.uniform(key_of[5], (LOGIT_PARTS, HEADS), jnp.float32) ** steps_of(key_of[5], (LOGIT_PARTS, HEADS), ((0, 4),), -0.2, 0.2)), 20.0, 400.0)
    return dict(grad_partials=grad_partials, assignment=assignment, momentum=momentum, q_weight=q_weight, k_weight=k_weight, max_logits=max_logits)


MOMENTUM_RATE = 0.95
WEIGHT_KEEP = 0.98
LOGIT_CAP = 100.0
QUINTIC_A = 3.4445
QUINTIC_B = -4.775
QUINTIC_C = 2.0315

def routing(assignment, heads_own, per_source):
    target = assignment[:, 0]
    head_index = jnp.arange(target.shape[0], dtype=jnp.int32)
    source_block = head_index // heads_own
    earlier = (source_block[None, :] == source_block[:, None]) & (head_index[None, :] < head_index[:, None]) & (target[None, :] == target[:, None])
    position = lax.optimization_barrier(jnp.sum(earlier.astype(jnp.int32), axis=1)).astype(jnp.int32)
    return (target, position, (source_block * per_source + position).astype(jnp.int32))

def newton(matrix):
    square_sum = jnp.sum(matrix * matrix)
    iterate = (matrix / (jnp.sqrt(square_sum) + 1e-07)).astype(jnp.bfloat16)
    for step in range(ITERS):
        gram_matrix = jnp.dot(iterate.T, iterate, preferred_element_type=jnp.float32)
        polynomial = (QUINTIC_B * gram_matrix + QUINTIC_C * jnp.dot(gram_matrix, gram_matrix, precision=lax.Precision.HIGHEST)).astype(jnp.bfloat16)
        iterate = (QUINTIC_A * iterate.astype(jnp.float32) + jnp.dot(iterate, polynomial, preferred_element_type=jnp.float32)).astype(jnp.bfloat16)
    return iterate

def refresh(weight, orthogonal, gamma, kn_count):
    step_size = 0.04 * math.sqrt(max(QR, QK))
    column_index = jnp.arange(weight.shape[2])
    column_scale = jnp.where(column_index[None, :] < kn_count, jnp.sqrt(gamma)[:, None], gamma[:, None])
    return (WEIGHT_KEEP * weight - step_size * orthogonal.astype(jnp.float32)) * column_scale[:, None, :]

def reference(grad_partials, assignment, momentum, q_weight, k_weight, max_logits):

    def add_part(part_index, running):
        return running + lax.dynamic_index_in_dim(grad_partials, part_index, 0, keepdims=False).astype(jnp.float32)
    grad = lax.fori_loop(0, GRAD_PARTS, add_part, jnp.zeros((QR, HEADS, QK), jnp.float32))
    target, position, local_slot = routing(assignment, HEADS_OWN, C_SEND)
    slot = (target * SLOTS_OWN + local_slot).astype(jnp.int32)
    refreshed = MOMENTUM_RATE * momentum[slot] + jnp.transpose(grad, (1, 0, 2))
    momentum_out = momentum.at[slot].set(refreshed)
    orthogonal = lax.map(newton, refreshed)
    peak_logit = lax.optimization_barrier(jnp.max(max_logits, axis=0))
    gamma = jnp.minimum(1.0, LOGIT_CAP / peak_logit)
    q_weight_out = q_weight.at[slot].set(refresh(q_weight[slot], orthogonal, gamma, KN))
    k_weight_out = k_weight * jnp.sqrt(gamma)[:, None, None]
    return (momentum_out, q_weight_out, k_weight_out)
```

```python
import functools
import math

import jax
import jax.numpy as jnp
from jax import lax
from jax.experimental import pallas as pl
from jax.experimental.pallas import tpu as pltpu
from jax.sharding import PartitionSpec as P

QR = 1536
QK = 192
ITERS = 2
MOMENTUM_RATE = 0.95
WEIGHT_KEEP = 0.98
LOGIT_CAP = 100.0
QUINTIC_A = 3.4445
QUINTIC_B = -4.775
QUINTIC_C = 2.0315

MESH = pl.DeviceIdType.MESH
BLOCKS = 32
ROWS = QR // BLOCKS
OWNERS = 8
HEADS_OWN = 8
SLOTS_OWN = 16
CHUNKS = 3
WIDTH = QK // CHUNKS
F32 = jnp.float32
BF16 = jnp.bfloat16


def rem(a, n):
    return lax.rem(a, jnp.int32(n))


def div(a, n):
    return lax.div(a, jnp.int32(n))


def dot_f32(a, b):
    return jnp.dot(a, b, precision=lax.Precision.HIGHEST, preferred_element_type=F32)


def kernel(
    index, grad, momentum, weight, k_weight, logits, slot_mask,
    momentum_out, weight_out, k_out,
    raw, packed, relay, direct, sibling, forward, forwarded, part, cross, heads, outgoing, arrived,
    mom, wgt, kwt, peaks, send_a, send_b, rows_a, rows_b, result, back,
    load_sem, state_sem, store_sem, s1_sem, fw_sem, s2_sem, relay_sem, direct_sem, sibling_sem,
    forwarded_sem, cross_sem, z_send, z_recv, x_send, x_recv, b_send, b_recv, l_send, l_recv,
):
    dp, z, ctx = lax.axis_index("dp"), lax.axis_index("owner"), lax.axis_index("context")
    core, y = rem(ctx, 2), rem(dp, 4)
    x = div(ctx, 2) * 2 + div(dp, 4)
    me = dp * 4 + ctx
    chip = x * 4 + y

    def at(x, y, c):
        return {"dp": rem(x, 2) * 4 + y, "context": div(x, 2) * 2 + c}

    def block(b):
        return {"dp": div(b, 4), "context": rem(b, 4)}

    def ring(half):
        return (x, y) if half == 0 else (y, x)

    def ring_device(half, r, c):
        return at(r, y, c) if half == 0 else at(x, r, c)

    def cross_device(half, q):
        return at(x, q, core) if half == 0 else at(q, y, core)

    def remote(src, dst, send, recv, device):
        copy = pltpu.make_async_remote_copy(
            src_ref=src, dst_ref=dst, send_sem=send, recv_sem=recv, device_id=device, device_id_type=MESH
        )
        copy.start()

    def wait(ref, sem):
        pltpu.make_async_copy(ref, ref, sem).wait()

    for k in range(CHUNKS):
        pltpu.make_async_copy(grad.at[:, k * WIDTH : (k + 1) * WIDTH, :], raw.at[k], load_sem.at[k]).start()
    loads = [
        pltpu.make_async_copy(momentum, mom, state_sem.at[0]),
        pltpu.make_async_copy(weight, wgt, state_sem.at[1]),
        pltpu.make_async_copy(k_weight, kwt, state_sem.at[2]),
    ]
    for copy in loads:
        copy.start()

    barrier = pltpu.get_barrier_semaphore()

    def greet(i, carry):
        pl.semaphore_signal(barrier, inc=1, device_id=block(rem(me + i, BLOCKS)), device_id_type=MESH)
        return carry

    def greet_z(i, carry):
        pl.semaphore_signal(barrier, inc=1, device_id={"owner": rem(z + i, OWNERS)}, device_id_type=MESH)
        return carry

    lax.fori_loop(1, BLOCKS, greet, 0)
    lax.fori_loop(1, OWNERS, greet_z, 0)

    row_at = lax.broadcasted_iota(jnp.int32, (384, 384), 0)
    column_at = lax.broadcasted_iota(jnp.int32, (384, 384), 1)
    eye = (row_at == column_at).astype(BF16)

    def pack(k):
        wait(raw.at[k], load_sem.at[k])
        for half in range(2):
            for group in range(4):
                block_in = raw[k, 4 * half : 4 * half + 4, :, 384 * group : 384 * group + 384]
                turned = lax.dot_general(
                    eye, block_in.reshape(4 * WIDTH, 384), (((1,), (1,)), ((), ())), preferred_element_type=F32
                ).astype(BF16)
                for i in range(8):
                    b = 8 * group + i
                    c_to, y_to, x_to = b % 2, (b // 4) % 4, (b // 2) % 2 * 2 + b // 16
                    r_to, q_to = (x_to, y_to) if half == 0 else (y_to, x_to)
                    for sub in range(2):
                        packed[k, half, r_to, c_to, sub, q_to] = turned[
                            ROWS * i : ROWS * i + ROWS, 128 * sub : 128 * sub + 128
                        ]

    def start_relays(k):
        for half in range(2):
            r, _ = ring(half)
            up, down, far = rem(r + 1, 4), rem(r + 3, 4), rem(r + 2, 4)
            for c in range(2):
                remote(packed.at[k, half, far, c, 0], relay.at[k, half, 0, core], s1_sem.at[k, half],
                       relay_sem.at[k, half], ring_device(half, up, c))
                remote(packed.at[k, half, far, c, 1], relay.at[k, half, 1, core], s1_sem.at[k, half],
                       relay_sem.at[k, half], ring_device(half, down, c))
            other = 1 - core
            here = at(x, y, other)
            remote(packed.at[k, half, up, other, 0], sibling.at[k, half, 0], s1_sem.at[k, half],
                   sibling_sem.at[k, half], here)
            remote(packed.at[k, half, down, other, 1], sibling.at[k, half, 1], s1_sem.at[k, half],
                   sibling_sem.at[k, half], here)
            remote(packed.at[k, half, r, other], sibling.at[k, half, pl.ds(2, 2)], s1_sem.at[k, half],
                   sibling_sem.at[k, half], here)

    def start_directs(k):
        for half in range(2):
            r, _ = ring(half)
            up, down = rem(r + 1, 4), rem(r + 3, 4)
            for c in range(2):
                remote(packed.at[k, half, up, c, 1], direct.at[k, half, 0, core], s1_sem.at[k, half],
                       direct_sem.at[k, half], ring_device(half, up, c))
                remote(packed.at[k, half, down, c, 0], direct.at[k, half, 1, core], s1_sem.at[k, half],
                       direct_sem.at[k, half], ring_device(half, down, c))

    def start_forwards(k):
        for half in range(2):
            r, _ = ring(half)
            up, down = rem(r + 1, 4), rem(r + 3, 4)
            wait(sibling.at[k, half], sibling_sem.at[k, half])
            wait(relay.at[k, half], relay_sem.at[k, half])
            for way, to in ((0, up), (1, down)):
                forward[k, half, way] = (
                    packed[k, half, to, core, way].astype(F32)
                    + sibling[k, half, way].astype(F32)
                    + relay[k, half, way, 0].astype(F32)
                    + relay[k, half, way, 1].astype(F32)
                )
                remote(forward.at[k, half, way], forwarded.at[k, half, way], fw_sem.at[k, half],
                       forwarded_sem.at[k, half], ring_device(half, to, core))

    def start_cross(k):
        for half in range(2):
            r, q = ring(half)
            wait(direct.at[k, half], direct_sem.at[k, half])
            wait(forwarded.at[k, half], forwarded_sem.at[k, half])
            for sub in range(2):
                total = (
                    packed[k, half, r, core, sub].astype(F32)
                    + sibling[k, half, 2 + sub].astype(F32)
                    + forwarded[k, half, sub]
                    + direct[k, half, 1 - sub, 0].astype(F32)
                    + direct[k, half, 1 - sub, 1].astype(F32)
                )
                for to in range(4):
                    part[k, half, to, sub] = total[to]
            for i in range(3):
                to = rem(q + 1 + i, 4)
                remote(part.at[k, half, to], cross.at[k, half, i], s2_sem.at[k, half],
                       cross_sem.at[k, half], cross_device(half, to))

    lane = lax.broadcasted_iota(jnp.int32, (ROWS, 128), 1)
    heads[HEADS_OWN] = jnp.zeros((ROWS, 128), F32)

    def start_owner(k):
        for half in range(2):
            _, q = ring(half)
            wait(cross.at[k, half], cross_sem.at[k, half])
            for sub in range(2):
                total = (
                    part[k, half, q, sub]
                    + cross[k, half, 0, sub]
                    + cross[k, half, 1, sub]
                    + cross[k, half, 2, sub]
                )
                pair = 2 * half + sub
                heads[2 * pair] = total
                heads[2 * pair + 1] = pltpu.roll(total, 64, 1)

        def fill(t, carry):
            outgoing[k, t] = jnp.where(lane < 64, heads[index[t]], heads[index[OWNERS + t]])
            return carry

        lax.fori_loop(0, OWNERS, fill, 0)
        for i in range(1, OWNERS):
            to = rem(z + i, OWNERS)
            remote(outgoing.at[k, to], arrived.at[k, z], z_send.at[k], z_recv.at[k], {"owner": to})
        arrived[k, z] = outgoing[k, z]

    def wait_owner(k):
        wait(arrived.at[k, pl.ds(0, OWNERS - 1)], z_recv.at[k])

    def start_rows(stage, source, target):
        def send(s, carry):
            mine = jnp.logical_and(s == chip, core == 0)

            @pl.when(jnp.logical_not(mine))
            def _():
                remote(source.at[s], target.at[me], x_send.at[stage], x_recv.at[stage], at(div(s, 4), rem(s, 4), 0))

            return carry

        lax.fori_loop(0, SLOTS_OWN, send, 0)

        @pl.when(core == 0)
        def _():
            target[me] = source[chip]

    pack(0)
    pl.semaphore_wait(barrier, BLOCKS - 1 + OWNERS - 1)
    start_relays(0)
    start_directs(0)
    peaks[ctx] = logits[...]
    for i in range(1, 4):
        remote(logits, peaks.at[ctx], l_send, l_recv, {"context": rem(ctx + i, 4)})
    pack(1)
    start_forwards(0)
    start_relays(1)
    start_directs(1)
    pack(2)
    start_cross(0)
    start_forwards(1)
    start_relays(2)
    start_directs(2)

    wait(peaks.at[pl.ds(0, 3)], l_recv)
    gamma = jnp.minimum(1.0, LOGIT_CAP / jnp.max(peaks[...], axis=0))
    occupied = jnp.sum(slot_mask[...], axis=1, keepdims=True) > 0.5
    slot_gamma = jnp.where(
        occupied, jnp.sum(slot_mask[...] * jnp.concatenate([gamma, gamma], axis=0), axis=1, keepdims=True), 1.0
    )
    rate = jnp.where(occupied, MOMENTUM_RATE, 1.0)
    keep = jnp.where(occupied, WEIGHT_KEEP, 1.0)
    step_size = jnp.where(occupied, 0.04 * math.sqrt(max(QR, QK)), 0.0)
    slot_root = jnp.sqrt(slot_gamma)
    home = lax.broadcasted_iota(jnp.int32, (8, 128), 1) == lax.broadcasted_iota(jnp.int32, (8, 128), 0) + 8 * z
    home_root = jnp.sqrt(jnp.sum(jnp.where(home, gamma, 0.0), axis=1, keepdims=True))
    loads[2].wait()
    for h in range(HEADS_OWN):
        kwt[h] = kwt[h] * home_root[h : h + 1, :]
    k_copy = pltpu.make_async_copy(kwt, k_out, store_sem.at[0])
    k_copy.start()

    start_owner(0)
    start_cross(1)
    start_forwards(2)
    start_owner(1)
    start_cross(2)
    loads[0].wait()
    wait_owner(0)
    wait_owner(1)
    for s in range(SLOTS_OWN):
        low, high = arrived[0, s // 2], arrived[1, s // 2]
        if s % 2 == 0:
            got = jnp.where(lane < 64, low, pltpu.roll(high, 64, 1))
        else:
            got = jnp.where(lane < 64, pltpu.roll(low, 64, 1), high)
        value = mom[s, :, 0:128] * rate[s : s + 1, :] + got
        mom[s, :, 0:128] = value
        send_a[s] = value.astype(BF16)
    start_rows(0, send_a, rows_a)
    start_owner(2)
    wait_owner(2)
    for s in range(SLOTS_OWN):
        got = arrived[2, s // 2]
        if s % 2 == 1:
            got = pltpu.roll(got, 64, 1)
        value = mom[s, :, 128:192] * rate[s : s + 1, :] + got[:, 0:64]
        mom[s, :, 128:192] = value
        send_b[s] = value.astype(BF16)
    start_rows(1, send_b, rows_b)
    m_copy = pltpu.make_async_copy(mom, momentum_out, store_sem.at[1])
    m_copy.start()

    @pl.when(core == 0)
    def _():
        wait(rows_a.at[pl.ds(0, BLOCKS - 1)], x_recv.at[0])
        wait(rows_b.at[pl.ds(0, BLOCKS - 1)], x_recv.at[1])
        whole = jnp.concatenate([rows_a[...].reshape(QR, 128), rows_b[...].reshape(QR, 64)], axis=1)
        square = (((0,), (0,)), ((), ()))
        gram = lax.dot_general(whole, whole, square, preferred_element_type=F32)
        diagonal = lax.broadcasted_iota(jnp.int32, (QK, QK), 0) == lax.broadcasted_iota(jnp.int32, (QK, QK), 1)
        square_sum = jnp.sum(jnp.sum(jnp.where(diagonal, gram, 0.0), axis=0, keepdims=True), axis=1, keepdims=True)
        scale = 1.0 / (jnp.sqrt(square_sum) + 1e-07)
        gram = gram * scale * scale
        for step in range(ITERS):
            polynomial = (QUINTIC_B * gram + QUINTIC_C * dot_f32(gram, gram)).astype(BF16)
            product = jnp.dot(whole, polynomial, preferred_element_type=F32)
            total = QUINTIC_A * whole.astype(F32) + product
            if step == 0:
                total = total * scale
            whole = total.astype(BF16)
            if step < ITERS - 1:
                gram = lax.dot_general(whole, whole, square, preferred_element_type=F32)
        result[...] = whole.reshape(BLOCKS, ROWS, QK)

        def send(i, carry):
            b = rem(me + i, BLOCKS)
            remote(result.at[b], back.at[chip], b_send, b_recv, block(b))
            return carry

        lax.fori_loop(1, BLOCKS, send, 0)
        back[chip] = result[me]

    loads[1].wait()

    @pl.when(core == 0)
    def _():
        wait(back.at[pl.ds(0, SLOTS_OWN - 1)], b_recv)

    @pl.when(core == 1)
    def _():
        wait(back, b_recv)

    for s in range(SLOTS_OWN):
        fresh = wgt[s] * keep[s : s + 1, :] - step_size[s : s + 1, :] * back[s].astype(F32)
        wgt[s, :, 0:128] = fresh[:, 0:128] * slot_root[s : s + 1, :]
        wgt[s, :, 128:192] = fresh[:, 128:192] * slot_gamma[s : s + 1, :]
    w_copy = pltpu.make_async_copy(wgt, weight_out, store_sem.at[2])
    w_copy.start()

    for k in range(CHUNKS):
        for half in range(2):
            wait(packed.at[k, half, pl.ds(0, 3)], s1_sem.at[k, half])
            wait(forward.at[k, half], fw_sem.at[k, half])
            wait(part.at[k, half, pl.ds(0, 3)], s2_sem.at[k, half])
        wait(outgoing.at[k, pl.ds(0, OWNERS - 1)], z_send.at[k])
    wait(peaks.at[pl.ds(0, 3)], l_send)

    @pl.when(core == 0)
    def _():
        wait(send_a.at[pl.ds(0, SLOTS_OWN - 1)], x_send.at[0])
        wait(send_b.at[pl.ds(0, SLOTS_OWN - 1)], x_send.at[1])
        wait(result.at[pl.ds(0, BLOCKS - 1)], b_send)

    @pl.when(core == 1)
    def _():
        wait(send_a, x_send.at[0])
        wait(send_b, x_send.at[1])

    k_copy.wait()
    m_copy.wait()
    w_copy.wait()


def routing(assignment, heads_own, per_source):
    target = assignment[:, 0]
    head_index = jnp.arange(target.shape[0], dtype=jnp.int32)
    source_block = head_index // heads_own
    earlier = (
        (source_block[None, :] == source_block[:, None])
        & (head_index[None, :] < head_index[:, None])
        & (target[None, :] == target[:, None])
    )
    position = jnp.sum(earlier.astype(jnp.int32), axis=1)
    return (target, position, source_block * per_source + position)


def body(grad_partials, assignment, momentum, q_weight, k_weight, max_logits):
    heads_own = grad_partials.shape[2]
    slots_own = momentum.shape[0]
    per_source = slots_own // OWNERS
    my_owner = lax.axis_index("owner")
    target, position, local_slot = routing(assignment, heads_own, per_source)
    slot_index = jnp.arange(slots_own, dtype=jnp.int32)
    slot_mask = ((target[None, :] == my_owner) & (local_slot[None, :] == slot_index[:, None])).astype(F32)
    slot_mask = jnp.pad(slot_mask, ((0, 0), (0, 64)))
    home = jnp.arange(64, dtype=jnp.int32)
    mine = (home // heads_own == my_owner)[None, :] & (
        (target[None, :] == slot_index[:, None] % OWNERS) & (position[None, :] == slot_index[:, None] // OWNERS)
    )
    local = jnp.where(slot_index[:, None] < OWNERS, home[None, :] % heads_own, (home[None, :] % heads_own) ^ 1)
    index = heads_own + jnp.sum(jnp.where(mine, local - heads_own, 0), axis=1)
    logits = jnp.broadcast_to(jnp.pad(max_logits, ((0, 0), (0, 64)), constant_values=LOGIT_CAP), (8, 128))
    turned = jnp.transpose(grad_partials[0], (1, 2, 0))
    any_space = pl.BlockSpec(memory_space=pl.ANY)
    vmem = pl.BlockSpec(memory_space=pltpu.VMEM)
    dma = pltpu.SemaphoreType.DMA
    wide = (4, ROWS, 128)
    return pl.pallas_call(
        kernel,
        out_shape=(
            jax.ShapeDtypeStruct(momentum.shape, F32),
            jax.ShapeDtypeStruct(q_weight.shape, F32),
            jax.ShapeDtypeStruct(k_weight.shape, F32),
        ),
        in_specs=[pl.BlockSpec(memory_space=pltpu.SMEM)] + [any_space] * 4 + [vmem] * 2,
        out_specs=(any_space,) * 3,
        scratch_shapes=[
            pltpu.VMEM((CHUNKS, HEADS_OWN, WIDTH, QR), BF16),
            pltpu.VMEM((CHUNKS, 2, 4, 2, 2) + wide, BF16),
            pltpu.VMEM((CHUNKS, 2, 2, 2) + wide, BF16),
            pltpu.VMEM((CHUNKS, 2, 2, 2) + wide, BF16),
            pltpu.VMEM((CHUNKS, 2, 4) + wide, BF16),
            pltpu.VMEM((CHUNKS, 2, 2) + wide, F32),
            pltpu.VMEM((CHUNKS, 2, 2) + wide, F32),
            pltpu.VMEM((CHUNKS, 2, 4, 2, ROWS, 128), F32),
            pltpu.VMEM((CHUNKS, 2, 3, 2, ROWS, 128), F32),
            pltpu.VMEM((HEADS_OWN + 1, ROWS, 128), F32),
            pltpu.VMEM((CHUNKS, OWNERS, ROWS, 128), F32),
            pltpu.VMEM((CHUNKS, OWNERS, ROWS, 128), F32),
            pltpu.VMEM(momentum.shape, F32),
            pltpu.VMEM(q_weight.shape, F32),
            pltpu.VMEM(k_weight.shape, F32),
            pltpu.VMEM((4, 8, 128), F32),
            pltpu.VMEM((SLOTS_OWN, ROWS, 128), BF16),
            pltpu.VMEM((SLOTS_OWN, ROWS, 64), BF16),
            pltpu.VMEM((BLOCKS, ROWS, 128), BF16),
            pltpu.VMEM((BLOCKS, ROWS, 64), BF16),
            pltpu.VMEM((BLOCKS, ROWS, QK), BF16),
            pltpu.VMEM((SLOTS_OWN, ROWS, QK), BF16),
            dma((CHUNKS,)),
            dma((3,)),
            dma((3,)),
            dma((CHUNKS, 2)),
            dma((CHUNKS, 2)),
            dma((CHUNKS, 2)),
            dma((CHUNKS, 2)),
            dma((CHUNKS, 2)),
            dma((CHUNKS, 2)),
            dma((CHUNKS, 2)),
            dma((CHUNKS, 2)),
            dma((CHUNKS,)),
            dma((CHUNKS,)),
            dma((2,)),
            dma((2,)),
            dma,
            dma,
            dma,
            dma,
        ],
        compiler_params=pltpu.CompilerParams(
            collective_id=0, has_side_effects=True, vmem_limit_bytes=56 * 1024 * 1024
        ),
    )(index, turned, momentum, q_weight, k_weight, logits, slot_mask)


def solution(mesh):
    placed = (
        P(("dp", "context"), None, "owner", None),
        P(),
        P("owner", ("dp", "context"), None),
        P("owner", ("dp", "context"), None),
        P("owner", ("dp", "context"), None),
        P("context", None),
    )
    return jax.shard_map(
        body,
        mesh=mesh,
        in_specs=placed,
        out_specs=(
            P("owner", ("dp", "context"), None),
            P("owner", ("dp", "context"), None),
            P("owner", ("dp", "context"), None),
        ),
        check_vma=False,
    )
```

```python
import functools
import math

import jax
import jax.numpy as jnp
from jax import lax
from jax.experimental import pallas as pl
from jax.experimental.pallas import tpu as pltpu
from jax.sharding import PartitionSpec as P

QR = 1536
QK = 192
ITERS = 2
MOMENTUM_RATE = 0.95
WEIGHT_KEEP = 0.98
LOGIT_CAP = 100.0
QUINTIC_A = 3.4445
QUINTIC_B = -4.775
QUINTIC_C = 2.0315

MESH = pl.DeviceIdType.MESH
BLOCKS = 32
ROWS = QR // BLOCKS
OWNERS = 8
HEADS_OWN = 8
HEADS = 64
SLOTS_OWN = 16
CHUNKS = 3
WIDTH = QK // CHUNKS
F32 = jnp.float32
BF16 = jnp.bfloat16


def rem(a, n):
    return lax.rem(a, jnp.int32(n))


def div(a, n):
    return lax.div(a, jnp.int32(n))


def dot_f32(a, b):
    return jnp.dot(a, b, precision=lax.Precision.HIGHEST, preferred_element_type=F32)


def kernel(
    assignment, grad, momentum, weight, k_weight, logits,
    momentum_out, weight_out, k_out,
    mom, wgt, kwt, raw, packed, relay, direct, sibling, forward, forwarded, part, cross_relay, cross_direct, cross_forward,
    cross_forwarded, heads, outgoing, arrived, index, table, targets, logit_row, mine, peaks,
    send_a, send_b, rows_a, rows_b, result, back,
    load_sem, state_sem, s1_sem, fw_sem, s2_sem, relay_sem, direct_sem, sibling_sem, forwarded_sem,
    cross_relay_sem, cross_direct_sem, cross_forwarded_sem,
    z_send, z_recv, x_send, x_recv, b_send, b_recv, l_send, l_recv, store_sem,
):
    dp, z, ctx = lax.axis_index("dp"), lax.axis_index("owner"), lax.axis_index("context")
    core, y = rem(ctx, 2), rem(dp, 4)
    x = div(ctx, 2) * 2 + div(dp, 4)
    me = dp * 4 + ctx
    chip = x * 4 + y

    def at(x, y, c):
        return {"dp": rem(x, 2) * 4 + y, "context": div(x, 2) * 2 + c}

    def block(b):
        return {"dp": div(b, 4), "context": rem(b, 4)}

    def ring(half):
        return (x, y) if half == 0 else (y, x)

    def ring_device(half, r, c):
        return at(r, y, c) if half == 0 else at(x, r, c)

    def cross_device(half, q):
        return at(x, q, core) if half == 0 else at(q, y, core)

    def remote(src, dst, send, recv, device):
        copy = pltpu.make_async_remote_copy(
            src_ref=src, dst_ref=dst, send_sem=send, recv_sem=recv, device_id=device, device_id_type=MESH
        )
        copy.start()

    def wait(ref, sem):
        pltpu.make_async_copy(ref, ref, sem).wait()

    for k in range(CHUNKS):
        pltpu.make_async_copy(grad.at[:, k * WIDTH : (k + 1) * WIDTH, :], raw.at[k], load_sem.at[k]).start()
    loads = [
        pltpu.make_async_copy(momentum, mom, state_sem.at[0]),
        pltpu.make_async_copy(weight, wgt, state_sem.at[1]),
        pltpu.make_async_copy(k_weight, kwt, state_sem.at[2]),
        pltpu.make_async_copy(assignment, table, state_sem.at[3]),
        pltpu.make_async_copy(assignment, targets, state_sem.at[4]),
        pltpu.make_async_copy(logits, logit_row, state_sem.at[5]),
    ]
    for copy in loads:
        copy.start()

    barrier = pltpu.get_barrier_semaphore()

    def greet(i, carry):
        pl.semaphore_signal(barrier, inc=1, device_id=block(rem(me + i, BLOCKS)), device_id_type=MESH)
        return carry

    def greet_z(i, carry):
        pl.semaphore_signal(barrier, inc=1, device_id={"owner": rem(z + i, OWNERS)}, device_id_type=MESH)
        return carry

    lax.fori_loop(1, BLOCKS, greet, 0)
    lax.fori_loop(1, OWNERS, greet_z, 0)

    row_at = lax.broadcasted_iota(jnp.int32, (384, 384), 0)
    column_at = lax.broadcasted_iota(jnp.int32, (384, 384), 1)
    eye = (row_at == column_at).astype(BF16)

    def pack(k):
        wait(raw.at[k], load_sem.at[k])
        for half in range(2):
            for group in range(4):
                block_in = raw[k, 4 * half : 4 * half + 4, :, 384 * group : 384 * group + 384]
                turned = lax.dot_general(
                    eye, block_in.reshape(4 * WIDTH, 384), (((1,), (1,)), ((), ())), preferred_element_type=F32
                ).astype(BF16)
                for i in range(8):
                    b = 8 * group + i
                    c_to, y_to, x_to = b % 2, (b // 4) % 4, (b // 2) % 2 * 2 + b // 16
                    r_to, q_to = (x_to, y_to) if half == 0 else (y_to, x_to)
                    for sub in range(2):
                        packed[k, half, r_to, c_to, sub, q_to] = turned[
                            ROWS * i : ROWS * i + ROWS, 128 * sub : 128 * sub + 128
                        ]

    def start_relays(k):
        for half in range(2):
            r, _ = ring(half)
            up, down, far = rem(r + 1, 4), rem(r + 3, 4), rem(r + 2, 4)
            for c in range(2):
                remote(packed.at[k, half, far, c, 0], relay.at[k, half, 0, core], s1_sem.at[k, half],
                       relay_sem.at[k, half], ring_device(half, up, c))
                remote(packed.at[k, half, far, c, 1], relay.at[k, half, 1, core], s1_sem.at[k, half],
                       relay_sem.at[k, half], ring_device(half, down, c))
            other = 1 - core
            here = at(x, y, other)
            remote(packed.at[k, half, up, other, 0], sibling.at[k, half, 0], s1_sem.at[k, half],
                   sibling_sem.at[k, half], here)
            remote(packed.at[k, half, down, other, 1], sibling.at[k, half, 1], s1_sem.at[k, half],
                   sibling_sem.at[k, half], here)
            remote(packed.at[k, half, r, other], sibling.at[k, half, pl.ds(2, 2)], s1_sem.at[k, half],
                   sibling_sem.at[k, half], here)

    def start_directs(k):
        for half in range(2):
            r, _ = ring(half)
            up, down = rem(r + 1, 4), rem(r + 3, 4)
            for c in range(2):
                remote(packed.at[k, half, up, c, 1], direct.at[k, half, 0, core], s1_sem.at[k, half],
                       direct_sem.at[k, half], ring_device(half, up, c))
                remote(packed.at[k, half, down, c, 0], direct.at[k, half, 1, core], s1_sem.at[k, half],
                       direct_sem.at[k, half], ring_device(half, down, c))

    def start_forwards(k):
        for half in range(2):
            r, _ = ring(half)
            up, down = rem(r + 1, 4), rem(r + 3, 4)
            wait(sibling.at[k, half], sibling_sem.at[k, half])
            wait(relay.at[k, half], relay_sem.at[k, half])
            for way, to in ((0, up), (1, down)):
                forward[k, half, way] = (
                    packed[k, half, to, core, way].astype(F32)
                    + sibling[k, half, way].astype(F32)
                    + relay[k, half, way, 0].astype(F32)
                    + relay[k, half, way, 1].astype(F32)
                )
                remote(forward.at[k, half, way], forwarded.at[k, half, way], fw_sem.at[k, half],
                       forwarded_sem.at[k, half], ring_device(half, to, core))

    def start_cross(k):
        for half in range(2):
            r, q = ring(half)
            wait(direct.at[k, half], direct_sem.at[k, half])
            wait(forwarded.at[k, half], forwarded_sem.at[k, half])
            for sub in range(2):
                total = (
                    packed[k, half, r, core, sub].astype(F32)
                    + sibling[k, half, 2 + sub].astype(F32)
                    + forwarded[k, half, sub]
                    + direct[k, half, 1 - sub, 0].astype(F32)
                    + direct[k, half, 1 - sub, 1].astype(F32)
                )
                for to in range(4):
                    part[k, half, to, sub] = total[to]
            up, down, far = rem(q + 1, 4), rem(q + 3, 4), rem(q + 2, 4)
            for way, to in ((0, up), (1, down)):
                remote(part.at[k, half, far, way], cross_relay.at[k, half, way], s2_sem.at[k, half],
                       cross_relay_sem.at[k, half], cross_device(half, to))
            for way, to in ((0, up), (1, down)):
                remote(part.at[k, half, to, 1 - way], cross_direct.at[k, half, way], s2_sem.at[k, half],
                       cross_direct_sem.at[k, half], cross_device(half, to))

    def start_cross_forwards(k):
        for half in range(2):
            _, q = ring(half)
            up, down = rem(q + 1, 4), rem(q + 3, 4)
            wait(cross_relay.at[k, half], cross_relay_sem.at[k, half])
            for way, to in ((0, up), (1, down)):
                cross_forward[k, half, way] = part[k, half, to, way] + cross_relay[k, half, way]
                remote(cross_forward.at[k, half, way], cross_forwarded.at[k, half, way], s2_sem.at[k, half],
                       cross_forwarded_sem.at[k, half], cross_device(half, to))

    lane = lax.broadcasted_iota(jnp.int32, (ROWS, 128), 1)
    heads[HEADS_OWN] = jnp.zeros((ROWS, 128), F32)

    def start_owner(k):
        for half in range(2):
            _, q = ring(half)
            wait(cross_direct.at[k, half], cross_direct_sem.at[k, half])
            wait(cross_forwarded.at[k, half], cross_forwarded_sem.at[k, half])
            for sub in range(2):
                total = part[k, half, q, sub] + cross_forwarded[k, half, sub] + cross_direct[k, half, 1 - sub]
                pair = 2 * half + sub
                heads[2 * pair] = total
                heads[2 * pair + 1] = pltpu.roll(total, 64, 1)

        def fill(t, carry):
            outgoing[k, t] = jnp.where(lane < 64, heads[index[t]], heads[index[OWNERS + t]])
            return carry

        lax.fori_loop(0, OWNERS, fill, 0)
        for i in range(1, OWNERS):
            to = rem(z + i, OWNERS)
            remote(outgoing.at[k, to], arrived.at[k, z], z_send.at[k], z_recv.at[k], {"owner": to})
        arrived[k, z] = outgoing[k, z]

    def wait_owner(k):
        wait(arrived.at[k, pl.ds(0, OWNERS - 1)], z_recv.at[k])

    def start_rows(stage, source, target):
        def send(s, carry):
            mine = jnp.logical_and(s == chip, core == 0)

            @pl.when(jnp.logical_not(mine))
            def _():
                remote(source.at[s], target.at[me], x_send.at[stage], x_recv.at[stage], at(div(s, 4), rem(s, 4), 0))

            return carry

        lax.fori_loop(0, SLOTS_OWN, send, 0)

        @pl.when(core == 0)
        def _():
            target[me] = source[chip]

    pack(0)
    pl.semaphore_wait(barrier, BLOCKS - 1 + OWNERS - 1)
    start_relays(0)
    start_directs(0)
    loads[5].wait()
    row = logit_row[...]
    mine[...] = jnp.broadcast_to(jnp.concatenate([row, row], axis=1), (8, 128))
    peaks[ctx] = mine[...]
    for i in range(1, 4):
        remote(mine, peaks.at[ctx], l_send, l_recv, {"context": rem(ctx + i, 4)})
    pack(1)
    start_forwards(0)
    start_relays(1)
    start_directs(1)
    pack(2)
    start_cross(0)
    start_forwards(1)
    start_relays(2)
    start_directs(2)
    start_cross_forwards(0)

    loads[3].wait()
    named = [table[0, HEADS_OWN * z + i] for i in range(HEADS_OWN)]
    for t in range(OWNERS):
        first, beside, second = jnp.int32(HEADS_OWN), jnp.int32(HEADS_OWN), jnp.int32(HEADS_OWN)
        for i in reversed(range(HEADS_OWN)):
            hit = named[i] == t
            second = jnp.where(hit, beside, second)
            beside = jnp.where(hit, i ^ 1, beside)
            first = jnp.where(hit, i, first)
        index[t] = first
        index[OWNERS + t] = second

    loads[4].wait()
    along = jnp.broadcast_to(targets[...].astype(F32), (HEADS, HEADS))
    head_row = lax.broadcasted_iota(jnp.int32, (HEADS, HEADS), 0)
    head_lane = lax.broadcasted_iota(jnp.int32, (HEADS, HEADS), 1)
    down_column = jnp.sum(jnp.where(head_row == head_lane, along, 0.0), axis=1, keepdims=True)
    earlier = (down_column == along) & (div(head_row, 8) == div(head_lane, 8)) & (head_row < head_lane)
    position = jnp.sum(jnp.where(earlier, 1.0, 0.0), axis=0, keepdims=True)
    slot_row = lax.broadcasted_iota(jnp.int32, (SLOTS_OWN, HEADS), 0)
    slot_lane = lax.broadcasted_iota(jnp.int32, (SLOTS_OWN, HEADS), 1)
    in_slot = (along[0:SLOTS_OWN] == z.astype(F32)) & (
        (div(slot_lane, 8) * 2).astype(F32) + position == slot_row.astype(F32)
    )
    wait(peaks.at[pl.ds(0, 3)], l_recv)
    gamma = jnp.minimum(1.0, LOGIT_CAP / jnp.max(peaks[...], axis=0))
    occupied = jnp.sum(jnp.where(in_slot, 1.0, 0.0), axis=1, keepdims=True) > 0.5
    slot_gamma = jnp.where(
        occupied, jnp.sum(jnp.where(in_slot, gamma[0:1, 0:HEADS], 0.0), axis=1, keepdims=True), 1.0
    )
    rate = jnp.where(occupied, MOMENTUM_RATE, 1.0)
    keep = jnp.where(occupied, WEIGHT_KEEP, 1.0)
    step_size = jnp.where(occupied, 0.04 * math.sqrt(max(QR, QK)), 0.0)
    slot_root = jnp.sqrt(slot_gamma)
    home = lax.broadcasted_iota(jnp.int32, (8, 128), 1) == lax.broadcasted_iota(jnp.int32, (8, 128), 0) + 8 * z
    home_root = jnp.sqrt(jnp.sum(jnp.where(home, gamma, 0.0), axis=1, keepdims=True))
    loads[2].wait()
    for h in range(HEADS_OWN):
        kwt[h] = kwt[h] * home_root[h : h + 1, :]
    stores = [
        pltpu.make_async_copy(mom, momentum_out, store_sem.at[0]),
        pltpu.make_async_copy(wgt, weight_out, store_sem.at[1]),
        pltpu.make_async_copy(kwt, k_out, store_sem.at[2]),
    ]
    stores[2].start()

    start_cross(1)
    start_forwards(2)
    start_owner(0)
    start_cross_forwards(1)
    start_cross(2)
    start_owner(1)
    start_cross_forwards(2)
    start_owner(2)
    loads[0].wait()
    wait_owner(0)
    wait_owner(1)
    for s in range(SLOTS_OWN):
        low, high = arrived[0, s // 2], arrived[1, s // 2]
        if s % 2 == 0:
            got = jnp.where(lane < 64, low, pltpu.roll(high, 64, 1))
        else:
            got = jnp.where(lane < 64, pltpu.roll(low, 64, 1), high)
        value = mom[s, :, 0:128] * rate[s : s + 1, :] + got
        mom[s, :, 0:128] = value
        send_a[s] = value.astype(BF16)
    start_rows(0, send_a, rows_a)
    wait_owner(2)
    for s in range(SLOTS_OWN):
        got = arrived[2, s // 2]
        if s % 2 == 1:
            got = pltpu.roll(got, 64, 1)
        value = mom[s, :, 128:192] * rate[s : s + 1, :] + got[:, 0:64]
        mom[s, :, 128:192] = value
        send_b[s] = jnp.concatenate([value[0:24], value[24:48]], axis=1).astype(BF16)
    start_rows(1, send_b, rows_b)
    stores[0].start()

    @pl.when(core == 0)
    def _():
        wait(rows_a.at[pl.ds(0, BLOCKS - 1)], x_recv.at[0])
        wait(rows_b.at[pl.ds(0, BLOCKS - 1)], x_recv.at[1])
        tail = rows_b[...].astype(F32)
        tail = jnp.concatenate([tail[:, :, 0:64], tail[:, :, 64:128]], axis=1).astype(BF16)
        whole = jnp.concatenate([rows_a[...].reshape(QR, 128), tail.reshape(QR, 64)], axis=1)
        square = (((0,), (0,)), ((), ()))
        gram = lax.dot_general(whole, whole, square, preferred_element_type=F32)
        diagonal = lax.broadcasted_iota(jnp.int32, (QK, QK), 0) == lax.broadcasted_iota(jnp.int32, (QK, QK), 1)
        square_sum = jnp.sum(jnp.sum(jnp.where(diagonal, gram, 0.0), axis=0, keepdims=True), axis=1, keepdims=True)
        scale = 1.0 / (jnp.sqrt(square_sum) + 1e-07)
        gram = gram * scale * scale
        for step in range(ITERS):
            polynomial = (QUINTIC_B * gram + QUINTIC_C * dot_f32(gram, gram)).astype(BF16)
            product = jnp.dot(whole, polynomial, preferred_element_type=F32)
            total = QUINTIC_A * whole.astype(F32) + product
            if step == 0:
                total = total * scale
            if step < ITERS - 1:
                whole = total.astype(BF16)
                gram = lax.dot_general(whole, whole, square, preferred_element_type=F32)
        result[:, 0:ROWS, :] = total[:, 0:128].astype(BF16).reshape(BLOCKS, ROWS, 128)
        tail = total[:, 128:192].reshape(BLOCKS, ROWS, 64)
        result[:, ROWS:72, :] = jnp.concatenate([tail[:, 0:24], tail[:, 24:48]], axis=2).astype(BF16)

        def send(i, carry):
            b = rem(me + i, BLOCKS)
            remote(result.at[b], back.at[chip], b_send, b_recv, block(b))
            return carry

        lax.fori_loop(1, BLOCKS, send, 0)
        back[chip] = result[me]

    loads[1].wait()

    @pl.when(core == 0)
    def _():
        wait(back.at[pl.ds(0, SLOTS_OWN - 1)], b_recv)

    @pl.when(core == 1)
    def _():
        wait(back, b_recv)

    for s in range(SLOTS_OWN):
        kept, taken = keep[s : s + 1, :], step_size[s : s + 1, :]
        fresh = back[s].astype(F32)
        wgt[s, :, 0:128] = (wgt[s, :, 0:128] * kept - taken * fresh[0:ROWS]) * slot_root[s : s + 1, :]
        tail = jnp.concatenate([fresh[ROWS:72, 0:64], fresh[ROWS:72, 64:128]], axis=0)
        wgt[s, :, 128:192] = (wgt[s, :, 128:192] * kept - taken * tail) * slot_gamma[s : s + 1, :]

    stores[1].start()

    for k in range(CHUNKS):
        for half in range(2):
            wait(packed.at[k, half, pl.ds(0, 3)], s1_sem.at[k, half])
            wait(forward.at[k, half], fw_sem.at[k, half])
            wait(part.at[k, half, pl.ds(0, 3)], s2_sem.at[k, half])
        wait(outgoing.at[k, pl.ds(0, OWNERS - 1)], z_send.at[k])
    wait(peaks.at[pl.ds(0, 3)], l_send)

    @pl.when(core == 0)
    def _():
        wait(send_a.at[pl.ds(0, SLOTS_OWN - 1)], x_send.at[0])
        wait(send_b.at[pl.ds(0, SLOTS_OWN - 1)], x_send.at[1])
        wait(result.at[pl.ds(0, BLOCKS - 1)], b_send)

    @pl.when(core == 1)
    def _():
        wait(send_a, x_send.at[0])
        wait(send_b, x_send.at[1])

    for copy in stores:
        copy.wait()


def place(mom, wgt, kwt, momentum_out, weight_out, k_out, sem):
    copies = [
        pltpu.make_async_copy(mom, momentum_out, sem.at[0]),
        pltpu.make_async_copy(wgt, weight_out, sem.at[1]),
        pltpu.make_async_copy(kwt, k_out, sem.at[2]),
    ]
    for copy in copies:
        copy.start()
    for copy in copies:
        copy.wait()


def body(grad_partials, assignment, momentum, q_weight, k_weight, max_logits):
    turned = jnp.transpose(grad_partials[0], (1, 2, 0))
    hbm = pl.BlockSpec(memory_space=pltpu.HBM)
    vmem = pl.BlockSpec(memory_space=pltpu.VMEM)
    dma = pltpu.SemaphoreType.DMA
    wide = (4, ROWS, 128)
    outs = (
        jax.ShapeDtypeStruct(momentum.shape, F32),
        jax.ShapeDtypeStruct(q_weight.shape, F32),
        jax.ShapeDtypeStruct(k_weight.shape, F32),
    )
    made = pl.pallas_call(
        kernel,
        out_shape=outs,
        in_specs=[hbm] * 6,
        out_specs=(hbm,) * 3,
        scratch_shapes=[
            pltpu.VMEM(momentum.shape, F32),
            pltpu.VMEM(q_weight.shape, F32),
            pltpu.VMEM(k_weight.shape, F32),
            pltpu.VMEM((CHUNKS, HEADS_OWN, WIDTH, QR), BF16),
            pltpu.VMEM((CHUNKS, 2, 4, 2, 2) + wide, BF16),
            pltpu.VMEM((CHUNKS, 2, 2, 2) + wide, BF16),
            pltpu.VMEM((CHUNKS, 2, 2, 2) + wide, BF16),
            pltpu.VMEM((CHUNKS, 2, 4) + wide, BF16),
            pltpu.VMEM((CHUNKS, 2, 2) + wide, F32),
            pltpu.VMEM((CHUNKS, 2, 2) + wide, F32),
            pltpu.VMEM((CHUNKS, 2, 4, 2, ROWS, 128), F32),
            pltpu.VMEM((CHUNKS, 2, 2, ROWS, 128), F32),
            pltpu.VMEM((CHUNKS, 2, 2, ROWS, 128), F32),
            pltpu.VMEM((CHUNKS, 2, 2, ROWS, 128), F32),
            pltpu.VMEM((CHUNKS, 2, 2, ROWS, 128), F32),
            pltpu.VMEM((HEADS_OWN + 1, ROWS, 128), F32),
            pltpu.VMEM((CHUNKS, OWNERS, ROWS, 128), F32),
            pltpu.VMEM((CHUNKS, OWNERS, ROWS, 128), F32),
            pltpu.SMEM((2 * OWNERS,), jnp.int32),
            pltpu.SMEM((1, HEADS), jnp.int32),
            pltpu.VMEM((1, HEADS), jnp.int32),
            pltpu.VMEM((1, HEADS), F32),
            pltpu.VMEM((8, 128), F32),
            pltpu.VMEM((4, 8, 128), F32),
            pltpu.VMEM((SLOTS_OWN, ROWS, 128), BF16),
            pltpu.VMEM((SLOTS_OWN, 24, 128), BF16),
            pltpu.VMEM((BLOCKS, ROWS, 128), BF16),
            pltpu.VMEM((BLOCKS, 24, 128), BF16),
            pltpu.VMEM((BLOCKS, 72, 128), BF16),
            pltpu.VMEM((SLOTS_OWN, 72, 128), BF16),
            dma((CHUNKS,)),
            dma((6,)),
        ]
        + [dma((CHUNKS, 2))] * 10
        + [dma((CHUNKS,)), dma((CHUNKS,)), dma((2,)), dma((2,)), dma, dma, dma, dma, dma((3,))],
        compiler_params=pltpu.CompilerParams(
            collective_id=0, has_side_effects=True, vmem_limit_bytes=56 * 1024 * 1024
        ),
    )(assignment.reshape(1, HEADS), turned, momentum, q_weight, k_weight, max_logits)
    return pl.pallas_call(
        place,
        out_shape=outs,
        in_specs=[vmem] * 3,
        out_specs=(hbm,) * 3,
        scratch_shapes=[dma((3,))],
    )(*made)


def solution(mesh):
    placed = (
        P(("dp", "context"), None, "owner", None),
        P(),
        P("owner", ("dp", "context"), None),
        P("owner", ("dp", "context"), None),
        P("owner", ("dp", "context"), None),
        P("context", None),
    )
    return jax.shard_map(
        body,
        mesh=mesh,
        in_specs=placed,
        out_specs=(
            P("owner", ("dp", "context"), None),
            P("owner", ("dp", "context"), None),
            P("owner", ("dp", "context"), None),
        ),
        check_vma=False,
    )
```

```python
import functools
import math

import jax
import jax.numpy as jnp
from jax import lax
from jax.experimental import pallas as pl
from jax.experimental.pallas import tpu as pltpu
from jax.sharding import PartitionSpec as P

QR = 1536
QK = 192
ITERS = 2
MOMENTUM_RATE = 0.95
WEIGHT_KEEP = 0.98
LOGIT_CAP = 100.0
QUINTIC_A = 3.4445
QUINTIC_B = -4.775
QUINTIC_C = 2.0315

MESH = pl.DeviceIdType.MESH
BLOCKS = 32
ROWS = QR // BLOCKS
OWNERS = 8
HEADS_OWN = 8
HEADS = 64
SLOTS_OWN = 16
CHUNKS = 3
WIDTH = QK // CHUNKS
F32 = jnp.float32
BF16 = jnp.bfloat16


def rem(a, n):
    return lax.rem(a, jnp.int32(n))


def div(a, n):
    return lax.div(a, jnp.int32(n))


def dot_f32(a, b):
    return jnp.dot(a, b, precision=lax.Precision.HIGHEST, preferred_element_type=F32)


def kernel(
    assignment, grad, momentum, k_weight, logits,
    momentum_out, k_out, scale_out, back,
    mom, kwt, scales, raw, packed, relay, direct, sibling, forward, forwarded, part, cross_relay, cross_direct, cross_forward,
    cross_forwarded, heads, outgoing, arrived, index, table, targets, logit_row, mine, peaks,
    send_a, send_b, rows_a, rows_b, gram_mine, gram_other, iterate, result,
    load_sem, state_sem, s1_sem, fw_sem, s2_sem, relay_sem, direct_sem, sibling_sem, forwarded_sem,
    cross_relay_sem, cross_direct_sem, cross_forwarded_sem,
    z_send, z_recv, x_send, x_recv, g_send, g_recv, b_send, b_recv, l_send, l_recv, store_sem,
):
    dp, z, ctx = lax.axis_index("dp"), lax.axis_index("owner"), lax.axis_index("context")
    core, y = rem(ctx, 2), rem(dp, 4)
    x = div(ctx, 2) * 2 + div(dp, 4)
    me = dp * 4 + ctx
    chip = x * 4 + y

    def at(x, y, c):
        return {"dp": rem(x, 2) * 4 + y, "context": div(x, 2) * 2 + c}

    def block(b):
        return {"dp": div(b, 4), "context": rem(b, 4)}

    def ring(half):
        return (x, y) if half == 0 else (y, x)

    def ring_device(half, r, c):
        return at(r, y, c) if half == 0 else at(x, r, c)

    def cross_device(half, q):
        return at(x, q, core) if half == 0 else at(q, y, core)

    def remote(src, dst, send, recv, device):
        copy = pltpu.make_async_remote_copy(
            src_ref=src, dst_ref=dst, send_sem=send, recv_sem=recv, device_id=device, device_id_type=MESH
        )
        copy.start()

    def wait(ref, sem):
        pltpu.make_async_copy(ref, ref, sem).wait()

    for k in range(CHUNKS):
        pltpu.make_async_copy(grad.at[:, k * WIDTH : (k + 1) * WIDTH, :], raw.at[k], load_sem.at[k]).start()
    loads = [
        pltpu.make_async_copy(momentum, mom, state_sem.at[0]),
        pltpu.make_async_copy(k_weight, kwt, state_sem.at[1]),
        pltpu.make_async_copy(assignment, table, state_sem.at[2]),
        pltpu.make_async_copy(assignment, targets, state_sem.at[3]),
        pltpu.make_async_copy(logits, logit_row, state_sem.at[4]),
    ]
    for copy in loads:
        copy.start()

    barrier = pltpu.get_barrier_semaphore()

    def greet(i, carry):
        pl.semaphore_signal(barrier, inc=1, device_id=block(rem(me + i, BLOCKS)), device_id_type=MESH)
        return carry

    def greet_z(i, carry):
        pl.semaphore_signal(barrier, inc=1, device_id={"owner": rem(z + i, OWNERS)}, device_id_type=MESH)
        return carry

    lax.fori_loop(1, BLOCKS, greet, 0)
    lax.fori_loop(1, OWNERS, greet_z, 0)

    row_at = lax.broadcasted_iota(jnp.int32, (384, 384), 0)
    column_at = lax.broadcasted_iota(jnp.int32, (384, 384), 1)
    eye = (row_at == column_at).astype(BF16)

    def pack(k):
        wait(raw.at[k], load_sem.at[k])
        for half in range(2):
            for group in range(4):
                block_in = raw[k, 4 * half : 4 * half + 4, :, 384 * group : 384 * group + 384]
                turned = lax.dot_general(
                    eye, block_in.reshape(4 * WIDTH, 384), (((1,), (1,)), ((), ())), preferred_element_type=F32
                ).astype(BF16)
                for i in range(8):
                    b = 8 * group + i
                    c_to, y_to, x_to = b % 2, (b // 4) % 4, (b // 2) % 2 * 2 + b // 16
                    r_to, q_to = (x_to, y_to) if half == 0 else (y_to, x_to)
                    for sub in range(2):
                        packed[k, half, r_to, c_to, sub, q_to] = turned[
                            ROWS * i : ROWS * i + ROWS, 128 * sub : 128 * sub + 128
                        ]

    def start_relays(k):
        for half in range(2):
            r, _ = ring(half)
            up, down, far = rem(r + 1, 4), rem(r + 3, 4), rem(r + 2, 4)
            for c in range(2):
                remote(packed.at[k, half, far, c, 0], relay.at[k, half, 0, core], s1_sem.at[k, half],
                       relay_sem.at[k, half], ring_device(half, up, c))
                remote(packed.at[k, half, far, c, 1], relay.at[k, half, 1, core], s1_sem.at[k, half],
                       relay_sem.at[k, half], ring_device(half, down, c))
            other = 1 - core
            here = at(x, y, other)
            remote(packed.at[k, half, up, other, 0], sibling.at[k, half, 0], s1_sem.at[k, half],
                   sibling_sem.at[k, half], here)
            remote(packed.at[k, half, down, other, 1], sibling.at[k, half, 1], s1_sem.at[k, half],
                   sibling_sem.at[k, half], here)
            remote(packed.at[k, half, r, other], sibling.at[k, half, pl.ds(2, 2)], s1_sem.at[k, half],
                   sibling_sem.at[k, half], here)

    def start_directs(k):
        for half in range(2):
            r, _ = ring(half)
            up, down = rem(r + 1, 4), rem(r + 3, 4)
            for c in range(2):
                remote(packed.at[k, half, up, c, 1], direct.at[k, half, 0, core], s1_sem.at[k, half],
                       direct_sem.at[k, half], ring_device(half, up, c))
                remote(packed.at[k, half, down, c, 0], direct.at[k, half, 1, core], s1_sem.at[k, half],
                       direct_sem.at[k, half], ring_device(half, down, c))

    def start_forwards(k):
        for half in range(2):
            r, _ = ring(half)
            up, down = rem(r + 1, 4), rem(r + 3, 4)
            wait(sibling.at[k, half], sibling_sem.at[k, half])
            wait(relay.at[k, half], relay_sem.at[k, half])
            for way, to in ((0, up), (1, down)):
                forward[k, half, way] = (
                    packed[k, half, to, core, way].astype(F32)
                    + sibling[k, half, way].astype(F32)
                    + relay[k, half, way, 0].astype(F32)
                    + relay[k, half, way, 1].astype(F32)
                )
                remote(forward.at[k, half, way], forwarded.at[k, half, way], fw_sem.at[k, half],
                       forwarded_sem.at[k, half], ring_device(half, to, core))

    def start_cross(k):
        for half in range(2):
            r, q = ring(half)
            wait(direct.at[k, half], direct_sem.at[k, half])
            wait(forwarded.at[k, half], forwarded_sem.at[k, half])
            for sub in range(2):
                total = (
                    packed[k, half, r, core, sub].astype(F32)
                    + sibling[k, half, 2 + sub].astype(F32)
                    + forwarded[k, half, sub]
                    + direct[k, half, 1 - sub, 0].astype(F32)
                    + direct[k, half, 1 - sub, 1].astype(F32)
                )
                for to in range(4):
                    part[k, half, to, sub] = total[to]
            up, down, far = rem(q + 1, 4), rem(q + 3, 4), rem(q + 2, 4)
            for way, to in ((0, up), (1, down)):
                remote(part.at[k, half, far, way], cross_relay.at[k, half, way], s2_sem.at[k, half],
                       cross_relay_sem.at[k, half], cross_device(half, to))
            for way, to in ((0, up), (1, down)):
                remote(part.at[k, half, to, 1 - way], cross_direct.at[k, half, way], s2_sem.at[k, half],
                       cross_direct_sem.at[k, half], cross_device(half, to))

    def start_cross_forwards(k):
        for half in range(2):
            _, q = ring(half)
            up, down = rem(q + 1, 4), rem(q + 3, 4)
            wait(cross_relay.at[k, half], cross_relay_sem.at[k, half])
            for way, to in ((0, up), (1, down)):
                cross_forward[k, half, way] = part[k, half, to, way] + cross_relay[k, half, way]
                remote(cross_forward.at[k, half, way], cross_forwarded.at[k, half, way], s2_sem.at[k, half],
                       cross_forwarded_sem.at[k, half], cross_device(half, to))

    lane = lax.broadcasted_iota(jnp.int32, (ROWS, 128), 1)
    heads[HEADS_OWN] = jnp.zeros((ROWS, 128), F32)

    def start_owner(k):
        for half in range(2):
            _, q = ring(half)
            wait(cross_direct.at[k, half], cross_direct_sem.at[k, half])
            wait(cross_forwarded.at[k, half], cross_forwarded_sem.at[k, half])
            for sub in range(2):
                total = part[k, half, q, sub] + cross_forwarded[k, half, sub] + cross_direct[k, half, 1 - sub]
                pair = 2 * half + sub
                heads[2 * pair] = total
                heads[2 * pair + 1] = pltpu.roll(total, 64, 1)

        def fill(t, carry):
            outgoing[k, t] = jnp.where(lane < 64, heads[index[t]], heads[index[OWNERS + t]])
            return carry

        lax.fori_loop(0, OWNERS, fill, 0)
        for i in range(1, OWNERS):
            to = rem(z + i, OWNERS)
            remote(outgoing.at[k, to], arrived.at[k, z], z_send.at[k], z_recv.at[k], {"owner": to})
        arrived[k, z] = outgoing[k, z]

    def wait_owner(k):
        wait(arrived.at[k, pl.ds(0, OWNERS - 1)], z_recv.at[k])

    def start_rows(stage, source, target):
        def send(i, carry):
            s = rem(chip + i, SLOTS_OWN)
            remote(source.at[s], target.at[div(me, 2)], x_send.at[stage], x_recv.at[stage],
                   at(div(s, 4), rem(s, 4), core))
            return carry

        lax.fori_loop(1, SLOTS_OWN, send, 0)
        target[div(me, 2)] = source[chip]

    pack(0)
    pl.semaphore_wait(barrier, BLOCKS - 1 + OWNERS - 1)
    start_relays(0)
    pack(1)
    start_relays(1)
    start_directs(0)
    start_forwards(0)
    loads[4].wait()
    row = logit_row[...]
    mine[...] = jnp.broadcast_to(jnp.concatenate([row, row], axis=1), (8, 128))
    peaks[ctx] = mine[...]
    for i in range(1, 4):
        remote(mine, peaks.at[ctx], l_send, l_recv, {"context": rem(ctx + i, 4)})
    pack(2)
    start_relays(2)
    start_cross(0)
    start_directs(1)
    start_forwards(1)
    start_cross_forwards(0)
    start_directs(2)
    start_forwards(2)

    loads[2].wait()
    named = [table[0, HEADS_OWN * z + i] for i in range(HEADS_OWN)]
    for t in range(OWNERS):
        first, beside, second = jnp.int32(HEADS_OWN), jnp.int32(HEADS_OWN), jnp.int32(HEADS_OWN)
        for i in reversed(range(HEADS_OWN)):
            hit = named[i] == t
            second = jnp.where(hit, beside, second)
            beside = jnp.where(hit, i ^ 1, beside)
            first = jnp.where(hit, i, first)
        index[t] = first
        index[OWNERS + t] = second

    loads[3].wait()
    along = jnp.broadcast_to(targets[...].astype(F32), (HEADS, HEADS))
    head_row = lax.broadcasted_iota(jnp.int32, (HEADS, HEADS), 0)
    head_lane = lax.broadcasted_iota(jnp.int32, (HEADS, HEADS), 1)
    down_column = jnp.sum(jnp.where(head_row == head_lane, along, 0.0), axis=1, keepdims=True)
    earlier = (down_column == along) & (div(head_row, 8) == div(head_lane, 8)) & (head_row < head_lane)
    position = jnp.sum(jnp.where(earlier, 1.0, 0.0), axis=0, keepdims=True)
    slot_row = lax.broadcasted_iota(jnp.int32, (SLOTS_OWN, HEADS), 0)
    slot_lane = lax.broadcasted_iota(jnp.int32, (SLOTS_OWN, HEADS), 1)
    in_slot = (along[0:SLOTS_OWN] == z.astype(F32)) & (
        (div(slot_lane, 8) * 2).astype(F32) + position == slot_row.astype(F32)
    )
    wait(peaks.at[pl.ds(0, 3)], l_recv)
    gamma = jnp.minimum(1.0, LOGIT_CAP / jnp.max(peaks[...], axis=0))
    occupied = jnp.sum(jnp.where(in_slot, 1.0, 0.0), axis=1, keepdims=True) > 0.5
    slot_gamma = jnp.where(
        occupied, jnp.sum(jnp.where(in_slot, gamma[0:1, 0:HEADS], 0.0), axis=1, keepdims=True), 1.0
    )
    rate = jnp.where(occupied, MOMENTUM_RATE, 1.0)
    keep = jnp.where(occupied, WEIGHT_KEEP, 1.0)
    step_size = jnp.where(occupied, 0.04 * math.sqrt(max(QR, QK)), 0.0)
    slot_root = jnp.sqrt(slot_gamma)
    home = lax.broadcasted_iota(jnp.int32, (8, 128), 1) == lax.broadcasted_iota(jnp.int32, (8, 128), 0) + 8 * z
    home_root = jnp.sqrt(jnp.sum(jnp.where(home, gamma, 0.0), axis=1, keepdims=True))
    loads[1].wait()
    for h in range(HEADS_OWN):
        kwt[h] = kwt[h] * home_root[h : h + 1, :]
    stores = [
        pltpu.make_async_copy(mom, momentum_out, store_sem.at[0]),
        pltpu.make_async_copy(kwt, k_out, store_sem.at[1]),
        pltpu.make_async_copy(scales, scale_out, store_sem.at[2]),
    ]
    stores[1].start()
    scale_lane = lax.broadcasted_iota(jnp.int32, (SLOTS_OWN, 128), 1)
    scales[...] = jnp.where(
        scale_lane == 0, keep, jnp.where(scale_lane == 1, step_size, jnp.where(scale_lane == 2, slot_root, slot_gamma))
    )
    stores[2].start()

    start_owner(0)
    start_cross(1)
    start_cross_forwards(1)
    start_cross(2)
    start_owner(1)
    start_cross_forwards(2)
    start_owner(2)
    loads[0].wait()
    wait_owner(0)
    wait_owner(1)
    for s in range(SLOTS_OWN):
        low, high = arrived[0, s // 2], arrived[1, s // 2]
        if s % 2 == 0:
            got = jnp.where(lane < 64, low, pltpu.roll(high, 64, 1))
        else:
            got = jnp.where(lane < 64, pltpu.roll(low, 64, 1), high)
        value = mom[s, :, 0:128] * rate[s : s + 1, :] + got
        mom[s, :, 0:128] = value
        send_a[s] = value.astype(BF16)
    start_rows(0, send_a, rows_a)
    wait_owner(2)
    for s in range(SLOTS_OWN):
        got = arrived[2, s // 2]
        if s % 2 == 1:
            got = pltpu.roll(got, 64, 1)
        value = mom[s, :, 128:192] * rate[s : s + 1, :] + got[:, 0:64]
        mom[s, :, 128:192] = value
        send_b[s] = jnp.concatenate([value[0:24], value[24:48]], axis=1).astype(BF16)
    start_rows(1, send_b, rows_b)
    stores[0].start()

    others = pl.ds(0, SLOTS_OWN - 1)
    wait(rows_a.at[others], x_recv.at[0])
    wait(rows_b.at[others], x_recv.at[1])
    tail = rows_b[...].astype(F32)
    tail = jnp.concatenate([tail[:, :, 0:64], tail[:, :, 64:128]], axis=1).astype(BF16)
    whole = jnp.concatenate([rows_a[...].reshape(QR // 2, 128), tail.reshape(QR // 2, 64)], axis=1)
    gram_mine[...] = lax.dot_general(whole, whole, (((0,), (0,)), ((), ())), preferred_element_type=F32)
    remote(gram_mine, gram_other, g_send, g_recv, at(x, y, 1 - core))
    wait(gram_other, g_recv)
    gram = gram_mine[...] + gram_other[...]
    diagonal = lax.broadcasted_iota(jnp.int32, (QK, QK), 0) == lax.broadcasted_iota(jnp.int32, (QK, QK), 1)
    square_sum = jnp.sum(jnp.sum(jnp.where(diagonal, gram, 0.0), axis=0, keepdims=True), axis=1, keepdims=True)
    scale = 1.0 / (jnp.sqrt(square_sum) + 1e-07)
    gram = gram * scale * scale
    for step in range(ITERS - 1):
        polynomial = (QUINTIC_B * gram + QUINTIC_C * dot_f32(gram, gram)).astype(BF16)
        total = QUINTIC_A * whole.astype(F32) + jnp.dot(whole, polynomial, preferred_element_type=F32)
        if step == 0:
            total = total * scale
        whole = total.astype(BF16)
        factor = polynomial.astype(F32) + jnp.where(diagonal, QUINTIC_A, 0.0)
        gram = dot_f32(factor, dot_f32(gram, factor))
    iterate[...] = whole
    polynomial = (QUINTIC_B * gram + QUINTIC_C * dot_f32(gram, gram)).astype(BF16)

    def finish_group(n, carry):
        group = rem(n + x, 4)
        rows = iterate[pl.ds(pl.multiple_of(group * 192, 192), 192), :]
        total = QUINTIC_A * rows.astype(F32) + jnp.dot(rows, polynomial, preferred_element_type=F32)
        blocks = pl.ds(pl.multiple_of(group * 4, 4), 4)
        result[blocks, 0:ROWS, :] = total[:, 0:128].astype(BF16).reshape(4, ROWS, 128)
        tail = total[:, 128:192].reshape(4, ROWS, 64)
        result[blocks, ROWS:72, :] = jnp.concatenate([tail[:, 0:24], tail[:, 24:48]], axis=2).astype(BF16)

        def send(i, carry):
            j = group * 4 + rem(i + y, 4)
            b = 2 * j + core

            @pl.when(b != me)
            def _():
                remote(result.at[j], back.at[chip], b_send, b_recv, block(b))

            @pl.when(b == me)
            def _():
                pltpu.make_async_copy(result.at[j], back.at[chip], b_recv).start()

            return carry

        lax.fori_loop(0, 4, send, 0)
        return carry

    lax.fori_loop(0, 4, finish_group, 0)
    wait(back, b_recv)

    for k in range(CHUNKS):
        for half in range(2):
            wait(packed.at[k, half, pl.ds(0, 3)], s1_sem.at[k, half])
            wait(forward.at[k, half], fw_sem.at[k, half])
            wait(part.at[k, half, pl.ds(0, 3)], s2_sem.at[k, half])
        wait(outgoing.at[k, pl.ds(0, OWNERS - 1)], z_send.at[k])
    wait(peaks.at[pl.ds(0, 3)], l_send)

    wait(send_a.at[others], x_send.at[0])
    wait(send_b.at[others], x_send.at[1])
    wait(gram_mine, g_send)
    wait(result.at[others], b_send)
    for copy in stores:
        copy.wait()


def finish(
    made_momentum, made_k, made_scales, made_rows, weight,
    momentum_out, weight_out, k_out,
    mom, kwt, scales, rows, wgt, in_sem, row_sem, weight_sem, out_sem, weight_out_sem,
):
    groups = [pl.ds(4 * g, 4) for g in range(4)]
    scale_in = pltpu.make_async_copy(made_scales, scales, in_sem.at[0])
    scale_in.start()
    rows_in = [pltpu.make_async_copy(made_rows.at[g], rows.at[g], row_sem.at[i]) for i, g in enumerate(groups)]
    weight_in = [pltpu.make_async_copy(weight.at[g], wgt.at[g], weight_sem.at[i]) for i, g in enumerate(groups)]
    plain_in = [
        pltpu.make_async_copy(made_momentum, mom, in_sem.at[1]),
        pltpu.make_async_copy(made_k, kwt, in_sem.at[2]),
    ]
    plain_out = [
        pltpu.make_async_copy(mom, momentum_out, out_sem.at[0]),
        pltpu.make_async_copy(kwt, k_out, out_sem.at[1]),
    ]
    weight_back = [
        pltpu.make_async_copy(wgt.at[g], weight_out.at[g], weight_out_sem.at[i]) for i, g in enumerate(groups)
    ]
    for i in range(2):
        rows_in[i].start()
        weight_in[i].start()
    for copy in plain_in:
        copy.start()
    for i in range(2, 4):
        rows_in[i].start()
        weight_in[i].start()
    scale_in.wait()
    for i in range(4):
        if i == 2:
            for arriving, leaving in zip(plain_in, plain_out):
                arriving.wait()
                leaving.start()
        rows_in[i].wait()
        weight_in[i].wait()
        for s in range(4 * i, 4 * i + 4):
            kept, taken = scales[s : s + 1, 0:1], scales[s : s + 1, 1:2]
            root, gamma = scales[s : s + 1, 2:3], scales[s : s + 1, 3:4]
            fresh = rows[s].astype(F32)
            wgt[s, :, 0:128] = (wgt[s, :, 0:128] * kept - taken * fresh[0:ROWS]) * root
            tail = jnp.concatenate([fresh[ROWS:72, 0:64], fresh[ROWS:72, 64:128]], axis=0)
            wgt[s, :, 128:192] = (wgt[s, :, 128:192] * kept - taken * tail) * gamma
        weight_back[i].start()
    for copy in weight_back + plain_out:
        copy.wait()


def body(grad_partials, assignment, momentum, q_weight, k_weight, max_logits):
    turned = jnp.transpose(grad_partials[0], (1, 2, 0))
    hbm = pl.BlockSpec(memory_space=pltpu.HBM)
    vmem = pl.BlockSpec(memory_space=pltpu.VMEM)
    dma = pltpu.SemaphoreType.DMA
    wide = (4, ROWS, 128)
    momentum_like = jax.ShapeDtypeStruct(momentum.shape, F32)
    k_like = jax.ShapeDtypeStruct(k_weight.shape, F32)
    made = pl.pallas_call(
        kernel,
        out_shape=(
            momentum_like,
            k_like,
            jax.ShapeDtypeStruct((SLOTS_OWN, 128), F32),
            jax.ShapeDtypeStruct((SLOTS_OWN, 72, 128), BF16),
        ),
        in_specs=[hbm] * 5,
        out_specs=(hbm,) * 4,
        scratch_shapes=[
            pltpu.VMEM(momentum.shape, F32),
            pltpu.VMEM(k_weight.shape, F32),
            pltpu.VMEM((SLOTS_OWN, 128), F32),
            pltpu.VMEM((CHUNKS, HEADS_OWN, WIDTH, QR), BF16),
            pltpu.VMEM((CHUNKS, 2, 4, 2, 2) + wide, BF16),
            pltpu.VMEM((CHUNKS, 2, 2, 2) + wide, BF16),
            pltpu.VMEM((CHUNKS, 2, 2, 2) + wide, BF16),
            pltpu.VMEM((CHUNKS, 2, 4) + wide, BF16),
            pltpu.VMEM((CHUNKS, 2, 2) + wide, F32),
            pltpu.VMEM((CHUNKS, 2, 2) + wide, F32),
            pltpu.VMEM((CHUNKS, 2, 4, 2, ROWS, 128), F32),
            pltpu.VMEM((CHUNKS, 2, 2, ROWS, 128), F32),
            pltpu.VMEM((CHUNKS, 2, 2, ROWS, 128), F32),
            pltpu.VMEM((CHUNKS, 2, 2, ROWS, 128), F32),
            pltpu.VMEM((CHUNKS, 2, 2, ROWS, 128), F32),
            pltpu.VMEM((HEADS_OWN + 1, ROWS, 128), F32),
            pltpu.VMEM((CHUNKS, OWNERS, ROWS, 128), F32),
            pltpu.VMEM((CHUNKS, OWNERS, ROWS, 128), F32),
            pltpu.SMEM((2 * OWNERS,), jnp.int32),
            pltpu.SMEM((1, HEADS), jnp.int32),
            pltpu.VMEM((1, HEADS), jnp.int32),
            pltpu.VMEM((1, HEADS), F32),
            pltpu.VMEM((8, 128), F32),
            pltpu.VMEM((4, 8, 128), F32),
            pltpu.VMEM((SLOTS_OWN, ROWS, 128), BF16),
            pltpu.VMEM((SLOTS_OWN, 24, 128), BF16),
            pltpu.VMEM((SLOTS_OWN, ROWS, 128), BF16),
            pltpu.VMEM((SLOTS_OWN, 24, 128), BF16),
            pltpu.VMEM((QK, QK), F32),
            pltpu.VMEM((QK, QK), F32),
            pltpu.VMEM((QR // 2, QK), BF16),
            pltpu.VMEM((SLOTS_OWN, 72, 128), BF16),
            dma((CHUNKS,)),
            dma((5,)),
        ]
        + [dma((CHUNKS, 2))] * 10
        + [dma((CHUNKS,)), dma((CHUNKS,)), dma((2,)), dma((2,)), dma, dma, dma, dma, dma, dma, dma((3,))],
        compiler_params=pltpu.CompilerParams(
            collective_id=0, has_side_effects=True, vmem_limit_bytes=56 * 1024 * 1024
        ),
    )(assignment.reshape(1, HEADS), turned, momentum, k_weight, max_logits)
    return pl.pallas_call(
        finish,
        out_shape=(momentum_like, jax.ShapeDtypeStruct(q_weight.shape, F32), k_like),
        in_specs=[hbm] * 5,
        out_specs=(hbm,) * 3,
        scratch_shapes=[
            pltpu.VMEM(momentum.shape, F32),
            pltpu.VMEM(k_weight.shape, F32),
            pltpu.VMEM((SLOTS_OWN, 128), F32),
            pltpu.VMEM((SLOTS_OWN, 72, 128), BF16),
            pltpu.VMEM(q_weight.shape, F32),
            dma((3,)),
            dma((4,)),
            dma((4,)),
            dma((2,)),
            dma((4,)),
        ],
    )(*made, q_weight)


def solution(mesh):
    placed = (
        P(("dp", "context"), None, "owner", None),
        P(),
        P("owner", ("dp", "context"), None),
        P("owner", ("dp", "context"), None),
        P("owner", ("dp", "context"), None),
        P("context", None),
    )
    return jax.shard_map(
        body,
        mesh=mesh,
        in_specs=placed,
        out_specs=(
            P("owner", ("dp", "context"), None),
            P("owner", ("dp", "context"), None),
            P("owner", ("dp", "context"), None),
        ),
        check_vma=False,
    )
```

```python
import functools
import math

import jax
import jax.numpy as jnp
from jax import lax
from jax.experimental import pallas as pl
from jax.experimental.pallas import tpu as pltpu
from jax.sharding import PartitionSpec as P

QR = 1536
QK = 192
ITERS = 2
MOMENTUM_RATE = 0.95
WEIGHT_KEEP = 0.98
LOGIT_CAP = 100.0
QUINTIC_A = 3.4445
QUINTIC_B = -4.775
QUINTIC_C = 2.0315

MESH = pl.DeviceIdType.MESH
BLOCKS = 32
ROWS = QR // BLOCKS
OWNERS = 8
HEADS_OWN = 8
HEADS = 64
SLOTS_OWN = 16
CHUNKS = 3
WIDTH = QK // CHUNKS
F32 = jnp.float32
BF16 = jnp.bfloat16


def rem(a, n):
    return lax.rem(a, jnp.int32(n))


def div(a, n):
    return lax.div(a, jnp.int32(n))


def dot_f32(a, b):
    return jnp.dot(a, b, precision=lax.Precision.HIGHEST, preferred_element_type=F32)


def kernel(
    assignment, grad, momentum, k_weight, logits,
    momentum_out, k_out, scale_out, back,
    mom, kwt, scales, raw, packed, relay, direct, sibling, forward, forwarded, part, cross_relay, cross_direct, cross_forward,
    cross_forwarded, heads, outgoing, arrived, index, table, targets, logit_row, mine, peaks,
    send_a, send_b, rows_a, rows_b, gram_mine, gram_other, iterate, result,
    load_sem, state_sem, s1_sem, fw_sem, s2_sem, relay_sem, direct_sem, sibling_sem, forwarded_sem,
    cross_relay_sem, cross_direct_sem, cross_forwarded_sem,
    z_send, z_recv, x_send, x_recv, g_send, g_recv, b_send, b_recv, l_send, l_recv, store_sem,
):
    dp, z, ctx = lax.axis_index("dp"), lax.axis_index("owner"), lax.axis_index("context")
    core, y = rem(ctx, 2), rem(dp, 4)
    x = div(ctx, 2) * 2 + div(dp, 4)
    me = dp * 4 + ctx
    chip = x * 4 + y

    def at(x, y, c):
        return {"dp": rem(x, 2) * 4 + y, "context": div(x, 2) * 2 + c}

    def block(b):
        return {"dp": div(b, 4), "context": rem(b, 4)}

    def ring(half):
        return (x, y) if half == 0 else (y, x)

    def ring_device(half, r, c):
        return at(r, y, c) if half == 0 else at(x, r, c)

    def cross_device(half, q):
        return at(x, q, core) if half == 0 else at(q, y, core)

    def remote(src, dst, send, recv, device):
        copy = pltpu.make_async_remote_copy(
            src_ref=src, dst_ref=dst, send_sem=send, recv_sem=recv, device_id=device, device_id_type=MESH
        )
        copy.start()

    def wait(ref, sem):
        pltpu.make_async_copy(ref, ref, sem).wait()

    for k in range(CHUNKS):
        pltpu.make_async_copy(grad.at[:, k * WIDTH : (k + 1) * WIDTH, :], raw.at[k], load_sem.at[k]).start()
    loads = [
        pltpu.make_async_copy(momentum, mom, state_sem.at[0]),
        pltpu.make_async_copy(k_weight, kwt, state_sem.at[1]),
        pltpu.make_async_copy(assignment, table, state_sem.at[2]),
        pltpu.make_async_copy(assignment, targets, state_sem.at[3]),
        pltpu.make_async_copy(logits, logit_row, state_sem.at[4]),
    ]
    for copy in loads:
        copy.start()

    barrier = pltpu.get_barrier_semaphore()

    def greet(i, carry):
        pl.semaphore_signal(barrier, inc=1, device_id=block(rem(me + 2 * i, BLOCKS)), device_id_type=MESH)
        return carry

    def greet_z(i, carry):
        pl.semaphore_signal(barrier, inc=1, device_id={"owner": rem(z + i, OWNERS)}, device_id_type=MESH)
        return carry

    lax.fori_loop(1, BLOCKS // 2, greet, 0)
    beside = 1 - core
    near = (
        at(x, y, beside), at(rem(x + 1, 4), y, beside), at(rem(x + 3, 4), y, beside), at(rem(x + 2, 4), y, beside),
        at(x, rem(y + 1, 4), beside), at(x, rem(y + 3, 4), beside),
    )
    for device in near:
        pl.semaphore_signal(barrier, inc=1, device_id=device, device_id_type=MESH)
    lax.fori_loop(1, OWNERS, greet_z, 0)

    row_at = lax.broadcasted_iota(jnp.int32, (384, 384), 0)
    column_at = lax.broadcasted_iota(jnp.int32, (384, 384), 1)
    eye = (row_at == column_at).astype(BF16)

    def pack(k):
        wait(raw.at[k], load_sem.at[k])
        for half in range(2):
            for group in range(4):
                block_in = raw[k, 4 * half : 4 * half + 4, :, 384 * group : 384 * group + 384]
                turned = lax.dot_general(
                    eye, block_in.reshape(4 * WIDTH, 384), (((1,), (1,)), ((), ())), preferred_element_type=F32
                ).astype(BF16)
                for i in range(8):
                    b = 8 * group + i
                    c_to, y_to, x_to = b % 2, (b // 4) % 4, (b // 2) % 2 * 2 + b // 16
                    r_to, q_to = (x_to, y_to) if half == 0 else (y_to, x_to)
                    for sub in range(2):
                        packed[k, half, r_to, c_to, sub, q_to] = turned[
                            ROWS * i : ROWS * i + ROWS, 128 * sub : 128 * sub + 128
                        ]

    def start_relays(k):
        for half in range(2):
            r, _ = ring(half)
            up, down, far = rem(r + 1, 4), rem(r + 3, 4), rem(r + 2, 4)
            for c in range(2):
                remote(packed.at[k, half, far, c, 0], relay.at[k, half, 0, core], s1_sem.at[k, half],
                       relay_sem.at[k, half], ring_device(half, up, c))
                remote(packed.at[k, half, far, c, 1], relay.at[k, half, 1, core], s1_sem.at[k, half],
                       relay_sem.at[k, half], ring_device(half, down, c))
            other = 1 - core
            here = at(x, y, other)
            remote(packed.at[k, half, up, other, 0], sibling.at[k, half, 0], s1_sem.at[k, half],
                   sibling_sem.at[k, half], here)
            remote(packed.at[k, half, down, other, 1], sibling.at[k, half, 1], s1_sem.at[k, half],
                   sibling_sem.at[k, half], here)
            remote(packed.at[k, half, r, other], sibling.at[k, half, pl.ds(2, 2)], s1_sem.at[k, half],
                   sibling_sem.at[k, half], here)

    def start_directs(k):
        for half in range(2):
            r, _ = ring(half)
            up, down = rem(r + 1, 4), rem(r + 3, 4)
            for c in range(2):
                remote(packed.at[k, half, up, c, 1], direct.at[k, half, 0, core], s1_sem.at[k, half],
                       direct_sem.at[k, half], ring_device(half, up, c))
                remote(packed.at[k, half, down, c, 0], direct.at[k, half, 1, core], s1_sem.at[k, half],
                       direct_sem.at[k, half], ring_device(half, down, c))

    def start_forwards(k):
        for half in range(2):
            r, _ = ring(half)
            up, down = rem(r + 1, 4), rem(r + 3, 4)
            wait(sibling.at[k, half], sibling_sem.at[k, half])
            wait(relay.at[k, half], relay_sem.at[k, half])
            for way, to in ((0, up), (1, down)):
                forward[k, half, way] = (
                    packed[k, half, to, core, way].astype(F32)
                    + sibling[k, half, way].astype(F32)
                    + relay[k, half, way, 0].astype(F32)
                    + relay[k, half, way, 1].astype(F32)
                )
                remote(forward.at[k, half, way], forwarded.at[k, half, way], fw_sem.at[k, half],
                       forwarded_sem.at[k, half], ring_device(half, to, core))

    def start_cross(k):
        for half in range(2):
            r, q = ring(half)
            wait(direct.at[k, half], direct_sem.at[k, half])
            wait(forwarded.at[k, half], forwarded_sem.at[k, half])
            for sub in range(2):
                total = (
                    packed[k, half, r, core, sub].astype(F32)
                    + sibling[k, half, 2 + sub].astype(F32)
                    + forwarded[k, half, sub]
                    + direct[k, half, 1 - sub, 0].astype(F32)
                    + direct[k, half, 1 - sub, 1].astype(F32)
                )
                for to in range(4):
                    part[k, half, to, sub] = total[to]
            up, down, far = rem(q + 1, 4), rem(q + 3, 4), rem(q + 2, 4)
            for way, to in ((0, up), (1, down)):
                remote(part.at[k, half, far, way], cross_relay.at[k, half, way], s2_sem.at[k, half],
                       cross_relay_sem.at[k, half], cross_device(half, to))
            for way, to in ((0, up), (1, down)):
                remote(part.at[k, half, to, 1 - way], cross_direct.at[k, half, way], s2_sem.at[k, half],
                       cross_direct_sem.at[k, half], cross_device(half, to))

    def start_cross_forwards(k):
        for half in range(2):
            _, q = ring(half)
            up, down = rem(q + 1, 4), rem(q + 3, 4)
            wait(cross_relay.at[k, half], cross_relay_sem.at[k, half])
            for way, to in ((0, up), (1, down)):
                cross_forward[k, half, way] = part[k, half, to, way] + cross_relay[k, half, way]
                remote(cross_forward.at[k, half, way], cross_forwarded.at[k, half, way], s2_sem.at[k, half],
                       cross_forwarded_sem.at[k, half], cross_device(half, to))

    lane = lax.broadcasted_iota(jnp.int32, (ROWS, 128), 1)
    heads[HEADS_OWN] = jnp.zeros((ROWS, 128), F32)

    def start_owner(k):
        for half in range(2):
            _, q = ring(half)
            wait(cross_direct.at[k, half], cross_direct_sem.at[k, half])
            wait(cross_forwarded.at[k, half], cross_forwarded_sem.at[k, half])
            for sub in range(2):
                total = part[k, half, q, sub] + cross_forwarded[k, half, sub] + cross_direct[k, half, 1 - sub]
                pair = 2 * half + sub
                heads[2 * pair] = total
                heads[2 * pair + 1] = pltpu.roll(total, 64, 1)

        def fill(t, carry):
            outgoing[k, t] = jnp.where(lane < 64, heads[index[t]], heads[index[OWNERS + t]])
            return carry

        lax.fori_loop(0, OWNERS, fill, 0)
        for i in range(1, OWNERS):
            to = rem(z + i, OWNERS)
            remote(outgoing.at[k, to], arrived.at[k, z], z_send.at[k], z_recv.at[k], {"owner": to})
        arrived[k, z] = outgoing[k, z]

    def wait_owner(k):
        wait(arrived.at[k, pl.ds(0, OWNERS - 1)], z_recv.at[k])

    def start_rows(stage, source, target):
        def send(i, carry):
            s = rem(chip + i, SLOTS_OWN)
            remote(source.at[s], target.at[div(me, 2)], x_send.at[stage], x_recv.at[stage],
                   at(div(s, 4), rem(s, 4), core))
            return carry

        lax.fori_loop(1, SLOTS_OWN, send, 0)
        target[div(me, 2)] = source[chip]

    pack(0)
    pl.semaphore_wait(barrier, BLOCKS // 2 - 1 + len(near) + OWNERS - 1)
    start_relays(0)
    pack(1)
    start_relays(1)
    start_directs(0)
    start_forwards(0)
    loads[4].wait()
    row = logit_row[...]
    mine[...] = jnp.broadcast_to(jnp.concatenate([row, row], axis=1), (8, 128))
    peaks[ctx] = mine[...]
    for i in range(1, 4):
        remote(mine, peaks.at[ctx], l_send, l_recv, {"context": rem(ctx + i, 4)})
    pack(2)
    start_relays(2)
    start_cross(0)
    start_directs(1)
    start_forwards(1)
    start_cross_forwards(0)
    start_directs(2)
    start_forwards(2)

    loads[2].wait()
    named = [table[0, HEADS_OWN * z + i] for i in range(HEADS_OWN)]
    for t in range(OWNERS):
        first, beside, second = jnp.int32(HEADS_OWN), jnp.int32(HEADS_OWN), jnp.int32(HEADS_OWN)
        for i in reversed(range(HEADS_OWN)):
            hit = named[i] == t
            second = jnp.where(hit, beside, second)
            beside = jnp.where(hit, i ^ 1, beside)
            first = jnp.where(hit, i, first)
        index[t] = first
        index[OWNERS + t] = second

    loads[3].wait()
    along = jnp.broadcast_to(targets[...].astype(F32), (HEADS, HEADS))
    head_row = lax.broadcasted_iota(jnp.int32, (HEADS, HEADS), 0)
    head_lane = lax.broadcasted_iota(jnp.int32, (HEADS, HEADS), 1)
    down_column = jnp.sum(jnp.where(head_row == head_lane, along, 0.0), axis=1, keepdims=True)
    earlier = (down_column == along) & (div(head_row, 8) == div(head_lane, 8)) & (head_row < head_lane)
    position = jnp.sum(jnp.where(earlier, 1.0, 0.0), axis=0, keepdims=True)
    slot_row = lax.broadcasted_iota(jnp.int32, (SLOTS_OWN, HEADS), 0)
    slot_lane = lax.broadcasted_iota(jnp.int32, (SLOTS_OWN, HEADS), 1)
    in_slot = (along[0:SLOTS_OWN] == z.astype(F32)) & (
        (div(slot_lane, 8) * 2).astype(F32) + position == slot_row.astype(F32)
    )
    wait(peaks.at[pl.ds(0, 3)], l_recv)
    gamma = jnp.minimum(1.0, LOGIT_CAP / jnp.max(peaks[...], axis=0))
    occupied = jnp.sum(jnp.where(in_slot, 1.0, 0.0), axis=1, keepdims=True) > 0.5
    slot_gamma = jnp.where(
        occupied, jnp.sum(jnp.where(in_slot, gamma[0:1, 0:HEADS], 0.0), axis=1, keepdims=True), 1.0
    )
    rate = jnp.where(occupied, MOMENTUM_RATE, 1.0)
    keep = jnp.where(occupied, WEIGHT_KEEP, 1.0)
    step_size = jnp.where(occupied, 0.04 * math.sqrt(max(QR, QK)), 0.0)
    slot_root = jnp.sqrt(slot_gamma)
    home = lax.broadcasted_iota(jnp.int32, (8, 128), 1) == lax.broadcasted_iota(jnp.int32, (8, 128), 0) + 8 * z
    home_root = jnp.sqrt(jnp.sum(jnp.where(home, gamma, 0.0), axis=1, keepdims=True))
    loads[1].wait()
    for h in range(HEADS_OWN):
        kwt[h] = kwt[h] * home_root[h : h + 1, :]
    stores = [
        pltpu.make_async_copy(mom, momentum_out, store_sem.at[0]),
        pltpu.make_async_copy(kwt, k_out, store_sem.at[1]),
        pltpu.make_async_copy(scales, scale_out, store_sem.at[2]),
    ]
    stores[1].start()
    scale_lane = lax.broadcasted_iota(jnp.int32, (SLOTS_OWN, 128), 1)
    scales[...] = jnp.where(
        scale_lane == 0, keep, jnp.where(scale_lane == 1, step_size, jnp.where(scale_lane == 2, slot_root, slot_gamma))
    )
    stores[2].start()

    start_owner(0)
    start_cross(1)
    start_cross_forwards(1)
    start_cross(2)
    start_owner(1)
    start_cross_forwards(2)
    start_owner(2)
    loads[0].wait()
    wait_owner(0)
    wait_owner(1)
    for s in range(SLOTS_OWN):
        low, high = arrived[0, s // 2], arrived[1, s // 2]
        if s % 2 == 0:
            got = jnp.where(lane < 64, low, pltpu.roll(high, 64, 1))
        else:
            got = jnp.where(lane < 64, pltpu.roll(low, 64, 1), high)
        value = mom[s, :, 0:128] * rate[s : s + 1, :] + got
        mom[s, :, 0:128] = value
        send_a[s] = value.astype(BF16)
    start_rows(0, send_a, rows_a)
    wait_owner(2)
    for s in range(SLOTS_OWN):
        got = arrived[2, s // 2]
        if s % 2 == 1:
            got = pltpu.roll(got, 64, 1)
        value = mom[s, :, 128:192] * rate[s : s + 1, :] + got[:, 0:64]
        mom[s, :, 128:192] = value
        send_b[s] = jnp.concatenate([value[0:24], value[24:48]], axis=1).astype(BF16)
    start_rows(1, send_b, rows_b)
    stores[0].start()

    others = pl.ds(0, SLOTS_OWN - 1)
    wait(rows_a.at[others], x_recv.at[0])
    wait(rows_b.at[others], x_recv.at[1])
    tail = rows_b[...].astype(F32)
    tail = jnp.concatenate([tail[:, :, 0:64], tail[:, :, 64:128]], axis=1).astype(BF16)
    whole = jnp.concatenate([rows_a[...].reshape(QR // 2, 128), tail.reshape(QR // 2, 64)], axis=1)
    gram_mine[...] = lax.dot_general(whole, whole, (((0,), (0,)), ((), ())), preferred_element_type=F32)
    remote(gram_mine, gram_other, g_send, g_recv, at(x, y, 1 - core))
    wait(gram_other, g_recv)
    gram = gram_mine[...] + gram_other[...]
    diagonal = lax.broadcasted_iota(jnp.int32, (QK, QK), 0) == lax.broadcasted_iota(jnp.int32, (QK, QK), 1)
    square_sum = jnp.sum(jnp.sum(jnp.where(diagonal, gram, 0.0), axis=0, keepdims=True), axis=1, keepdims=True)
    scale = 1.0 / (jnp.sqrt(square_sum) + 1e-07)
    gram = gram * scale * scale
    for step in range(ITERS - 1):
        polynomial = (QUINTIC_B * gram + QUINTIC_C * dot_f32(gram, gram)).astype(BF16)
        total = QUINTIC_A * whole.astype(F32) + jnp.dot(whole, polynomial, preferred_element_type=F32)
        if step == 0:
            total = total * scale
        whole = total.astype(BF16)
        factor = polynomial.astype(F32) + jnp.where(diagonal, QUINTIC_A, 0.0)
        gram = dot_f32(factor, dot_f32(gram, factor))
    iterate[...] = whole
    polynomial = (QUINTIC_B * gram + QUINTIC_C * dot_f32(gram, gram)).astype(BF16)

    def finish_group(n, carry):
        group = rem(n + x, 4)
        rows = iterate[pl.ds(pl.multiple_of(group * 192, 192), 192), :]
        total = QUINTIC_A * rows.astype(F32) + jnp.dot(rows, polynomial, preferred_element_type=F32)
        blocks = pl.ds(pl.multiple_of(group * 4, 4), 4)
        result[blocks, 0:ROWS, :] = total[:, 0:128].astype(BF16).reshape(4, ROWS, 128)
        tail = total[:, 128:192].reshape(4, ROWS, 64)
        result[blocks, ROWS:72, :] = jnp.concatenate([tail[:, 0:24], tail[:, 24:48]], axis=2).astype(BF16)

        def send(i, carry):
            j = group * 4 + rem(i + y, 4)
            b = 2 * j + core

            @pl.when(b != me)
            def _():
                remote(result.at[j], back.at[chip], b_send, b_recv, block(b))

            @pl.when(b == me)
            def _():
                pltpu.make_async_copy(result.at[j], back.at[chip], b_recv).start()

            return carry

        lax.fori_loop(0, 4, send, 0)
        return carry

    lax.fori_loop(0, 4, finish_group, 0)
    wait(back, b_recv)

    for k in range(CHUNKS):
        for half in range(2):
            wait(packed.at[k, half, pl.ds(0, 3)], s1_sem.at[k, half])
            wait(forward.at[k, half], fw_sem.at[k, half])
            wait(part.at[k, half, pl.ds(0, 3)], s2_sem.at[k, half])
        wait(outgoing.at[k, pl.ds(0, OWNERS - 1)], z_send.at[k])
    wait(peaks.at[pl.ds(0, 3)], l_send)

    wait(send_a.at[others], x_send.at[0])
    wait(send_b.at[others], x_send.at[1])
    wait(gram_mine, g_send)
    wait(result.at[others], b_send)
    for copy in stores:
        copy.wait()


def finish(
    made_momentum, made_k, made_scales, made_rows, weight,
    momentum_out, weight_out, k_out,
    mom, kwt, scales, rows, wgt, in_sem, row_sem, weight_sem, out_sem, weight_out_sem,
):
    groups = [pl.ds(4 * g, 4) for g in range(4)]
    scale_in = pltpu.make_async_copy(made_scales, scales, in_sem.at[0])
    scale_in.start()
    rows_in = [pltpu.make_async_copy(made_rows.at[g], rows.at[g], row_sem.at[i]) for i, g in enumerate(groups)]
    weight_in = [pltpu.make_async_copy(weight.at[g], wgt.at[g], weight_sem.at[i]) for i, g in enumerate(groups)]
    plain_in = [
        pltpu.make_async_copy(made_momentum, mom, in_sem.at[1]),
        pltpu.make_async_copy(made_k, kwt, in_sem.at[2]),
    ]
    plain_out = [
        pltpu.make_async_copy(mom, momentum_out, out_sem.at[0]),
        pltpu.make_async_copy(kwt, k_out, out_sem.at[1]),
    ]
    weight_back = [
        pltpu.make_async_copy(wgt.at[g], weight_out.at[g], weight_out_sem.at[i]) for i, g in enumerate(groups)
    ]
    for i in range(2):
        rows_in[i].start()
        weight_in[i].start()
    for copy in plain_in:
        copy.start()
    for i in range(2, 4):
        rows_in[i].start()
        weight_in[i].start()
    scale_in.wait()
    for i in range(4):
        if i == 2:
            for arriving, leaving in zip(plain_in, plain_out):
                arriving.wait()
                leaving.start()
        rows_in[i].wait()
        weight_in[i].wait()
        for s in range(4 * i, 4 * i + 4):
            kept, taken = scales[s : s + 1, 0:1], scales[s : s + 1, 1:2]
            root, gamma = scales[s : s + 1, 2:3], scales[s : s + 1, 3:4]
            fresh = rows[s].astype(F32)
            wgt[s, :, 0:128] = (wgt[s, :, 0:128] * kept - taken * fresh[0:ROWS]) * root
            tail = jnp.concatenate([fresh[ROWS:72, 0:64], fresh[ROWS:72, 64:128]], axis=0)
            wgt[s, :, 128:192] = (wgt[s, :, 128:192] * kept - taken * tail) * gamma
        weight_back[i].start()
    for copy in weight_back + plain_out:
        copy.wait()


def body(grad_partials, assignment, momentum, q_weight, k_weight, max_logits):
    turned = jnp.transpose(grad_partials[0], (1, 2, 0))
    hbm = pl.BlockSpec(memory_space=pltpu.HBM)
    vmem = pl.BlockSpec(memory_space=pltpu.VMEM)
    dma = pltpu.SemaphoreType.DMA
    wide = (4, ROWS, 128)
    momentum_like = jax.ShapeDtypeStruct(momentum.shape, F32)
    k_like = jax.ShapeDtypeStruct(k_weight.shape, F32)
    made = pl.pallas_call(
        kernel,
        out_shape=(
            momentum_like,
            k_like,
            jax.ShapeDtypeStruct((SLOTS_OWN, 128), F32),
            jax.ShapeDtypeStruct((SLOTS_OWN, 72, 128), BF16),
        ),
        in_specs=[hbm] * 5,
        out_specs=(hbm,) * 4,
        scratch_shapes=[
            pltpu.VMEM(momentum.shape, F32),
            pltpu.VMEM(k_weight.shape, F32),
            pltpu.VMEM((SLOTS_OWN, 128), F32),
            pltpu.VMEM((CHUNKS, HEADS_OWN, WIDTH, QR), BF16),
            pltpu.VMEM((CHUNKS, 2, 4, 2, 2) + wide, BF16),
            pltpu.VMEM((CHUNKS, 2, 2, 2) + wide, BF16),
            pltpu.VMEM((CHUNKS, 2, 2, 2) + wide, BF16),
            pltpu.VMEM((CHUNKS, 2, 4) + wide, BF16),
            pltpu.VMEM((CHUNKS, 2, 2) + wide, F32),
            pltpu.VMEM((CHUNKS, 2, 2) + wide, F32),
            pltpu.VMEM((CHUNKS, 2, 4, 2, ROWS, 128), F32),
            pltpu.VMEM((CHUNKS, 2, 2, ROWS, 128), F32),
            pltpu.VMEM((CHUNKS, 2, 2, ROWS, 128), F32),
            pltpu.VMEM((CHUNKS, 2, 2, ROWS, 128), F32),
            pltpu.VMEM((CHUNKS, 2, 2, ROWS, 128), F32),
            pltpu.VMEM((HEADS_OWN + 1, ROWS, 128), F32),
            pltpu.VMEM((CHUNKS, OWNERS, ROWS, 128), F32),
            pltpu.VMEM((CHUNKS, OWNERS, ROWS, 128), F32),
            pltpu.SMEM((2 * OWNERS,), jnp.int32),
            pltpu.SMEM((1, HEADS), jnp.int32),
            pltpu.VMEM((1, HEADS), jnp.int32),
            pltpu.VMEM((1, HEADS), F32),
            pltpu.VMEM((8, 128), F32),
            pltpu.VMEM((4, 8, 128), F32),
            pltpu.VMEM((SLOTS_OWN, ROWS, 128), BF16),
            pltpu.VMEM((SLOTS_OWN, 24, 128), BF16),
            pltpu.VMEM((SLOTS_OWN, ROWS, 128), BF16),
            pltpu.VMEM((SLOTS_OWN, 24, 128), BF16),
            pltpu.VMEM((QK, QK), F32),
            pltpu.VMEM((QK, QK), F32),
            pltpu.VMEM((QR // 2, QK), BF16),
            pltpu.VMEM((SLOTS_OWN, 72, 128), BF16),
            dma((CHUNKS,)),
            dma((5,)),
        ]
        + [dma((CHUNKS, 2))] * 10
        + [dma((CHUNKS,)), dma((CHUNKS,)), dma((2,)), dma((2,)), dma, dma, dma, dma, dma, dma, dma((3,))],
        compiler_params=pltpu.CompilerParams(
            collective_id=0, has_side_effects=True, vmem_limit_bytes=56 * 1024 * 1024
        ),
    )(assignment.reshape(1, HEADS), turned, momentum, k_weight, max_logits)
    return pl.pallas_call(
        finish,
        out_shape=(momentum_like, jax.ShapeDtypeStruct(q_weight.shape, F32), k_like),
        in_specs=[hbm] * 5,
        out_specs=(hbm,) * 3,
        scratch_shapes=[
            pltpu.VMEM(momentum.shape, F32),
            pltpu.VMEM(k_weight.shape, F32),
            pltpu.VMEM((SLOTS_OWN, 128), F32),
            pltpu.VMEM((SLOTS_OWN, 72, 128), BF16),
            pltpu.VMEM(q_weight.shape, F32),
            dma((3,)),
            dma((4,)),
            dma((4,)),
            dma((2,)),
            dma((4,)),
        ],
    )(*made, q_weight)


def solution(mesh):
    placed = (
        P(("dp", "context"), None, "owner", None),
        P(),
        P("owner", ("dp", "context"), None),
        P("owner", ("dp", "context"), None),
        P("owner", ("dp", "context"), None),
        P("context", None),
    )
    return jax.shard_map(
        body,
        mesh=mesh,
        in_specs=placed,
        out_specs=(
            P("owner", ("dp", "context"), None),
            P("owner", ("dp", "context"), None),
            P("owner", ("dp", "context"), None),
        ),
        check_vma=False,
    )
```

```python
import functools
import math

import jax
import jax.numpy as jnp
from jax import lax
from jax.experimental import pallas as pl
from jax.experimental.pallas import tpu as pltpu
from jax.sharding import PartitionSpec as P

QR = 1536
QK = 192
ITERS = 2
MOMENTUM_RATE = 0.95
WEIGHT_KEEP = 0.98
LOGIT_CAP = 100.0
QUINTIC_A = 3.4445
QUINTIC_B = -4.775
QUINTIC_C = 2.0315

MESH = pl.DeviceIdType.MESH
BLOCKS = 32
ROWS = QR // BLOCKS
OWNERS = 8
HEADS_OWN = 8
HEADS = 64
SLOTS_OWN = 16
CHUNKS = 3
WIDTH = QK // CHUNKS
F32 = jnp.float32
BF16 = jnp.bfloat16


def rem(a, n):
    return lax.rem(a, jnp.int32(n))


def div(a, n):
    return lax.div(a, jnp.int32(n))


def dot_f32(a, b):
    a_high, b_high = a.astype(BF16), b.astype(BF16)
    a_low, b_low = (a - a_high.astype(F32)).astype(BF16), (b - b_high.astype(F32)).astype(BF16)
    dot = functools.partial(jnp.dot, preferred_element_type=F32)
    return dot(a_high, b_high) + (dot(a_high, b_low) + dot(a_low, b_high))


def kernel(
    assignment, grad, momentum, k_weight, logits,
    momentum_out, k_out, scale_out, back,
    mom, kwt, scales, raw, packed, relay, direct, sibling, forward, forwarded, part, cross_relay, cross_direct, cross_forward,
    cross_forwarded, heads, outgoing, arrived, index, table, targets, logit_row, mine, peaks,
    send_a, send_b, rows_a, rows_b, gram_mine, gram_other, iterate, result,
    load_sem, state_sem, s1_sem, fw_sem, s2_sem, relay_sem, direct_sem, sibling_sem, forwarded_sem,
    cross_relay_sem, cross_direct_sem, cross_forwarded_sem,
    z_send, z_recv, x_send, x_recv, g_send, g_recv, b_send, b_recv, l_send, l_recv, store_sem,
):
    dp, z, ctx = lax.axis_index("dp"), lax.axis_index("owner"), lax.axis_index("context")
    core, y = rem(ctx, 2), rem(dp, 4)
    x = div(ctx, 2) * 2 + div(dp, 4)
    me = dp * 4 + ctx
    chip = x * 4 + y

    def at(x, y, c):
        return {"dp": rem(x, 2) * 4 + y, "context": div(x, 2) * 2 + c}

    def block(b):
        return {"dp": div(b, 4), "context": rem(b, 4)}

    def ring(half):
        return (x, y) if half == 0 else (y, x)

    def ring_device(half, r, c):
        return at(r, y, c) if half == 0 else at(x, r, c)

    def cross_device(half, q):
        return at(x, q, core) if half == 0 else at(q, y, core)

    def remote(src, dst, send, recv, device):
        copy = pltpu.make_async_remote_copy(
            src_ref=src, dst_ref=dst, send_sem=send, recv_sem=recv, device_id=device, device_id_type=MESH
        )
        copy.start()

    def wait(ref, sem):
        pltpu.make_async_copy(ref, ref, sem).wait()

    for k in range(CHUNKS):
        pltpu.make_async_copy(grad.at[:, k * WIDTH : (k + 1) * WIDTH, :], raw.at[k], load_sem.at[k]).start()
    loads = [
        pltpu.make_async_copy(momentum, mom, state_sem.at[0]),
        pltpu.make_async_copy(k_weight, kwt, state_sem.at[1]),
        pltpu.make_async_copy(assignment, table, state_sem.at[2]),
        pltpu.make_async_copy(assignment, targets, state_sem.at[3]),
        pltpu.make_async_copy(logits, logit_row, state_sem.at[4]),
    ]
    for copy in loads:
        copy.start()

    barrier = pltpu.get_barrier_semaphore()

    def greet_z(i, carry):
        pl.semaphore_signal(barrier, inc=1, device_id={"owner": rem(z + i, OWNERS)}, device_id_type=MESH)
        return carry

    beside = 1 - core
    near = [at(x, y, beside)]
    for c in range(2):
        near += [at(rem(x + i, 4), y, c) for i in (1, 2, 3)] + [at(x, rem(y + i, 4), c) for i in (1, 3)]
    for device in near:
        pl.semaphore_signal(barrier, inc=1, device_id=device, device_id_type=MESH)
    lax.fori_loop(1, OWNERS, greet_z, 0)

    row_at = lax.broadcasted_iota(jnp.int32, (384, 384), 0)
    column_at = lax.broadcasted_iota(jnp.int32, (384, 384), 1)
    eye = (row_at == column_at).astype(BF16)

    def pack(k):
        wait(raw.at[k], load_sem.at[k])
        for half in range(2):
            for group in range(4):
                block_in = raw[k, 4 * half : 4 * half + 4, :, 384 * group : 384 * group + 384]
                turned = lax.dot_general(
                    eye, block_in.reshape(4 * WIDTH, 384), (((1,), (1,)), ((), ())), preferred_element_type=F32
                ).astype(BF16)
                for i in range(8):
                    b = 8 * group + i
                    c_to, y_to, x_to = b % 2, (b // 4) % 4, (b // 2) % 2 * 2 + b // 16
                    r_to, q_to = (x_to, y_to) if half == 0 else (y_to, x_to)
                    for sub in range(2):
                        packed[k, half, r_to, c_to, sub, q_to] = turned[
                            ROWS * i : ROWS * i + ROWS, 128 * sub : 128 * sub + 128
                        ]

    def start_relays(k):
        for half in range(2):
            r, _ = ring(half)
            up, down, far = rem(r + 1, 4), rem(r + 3, 4), rem(r + 2, 4)
            for c in range(2):
                remote(packed.at[k, half, far, c, 0], relay.at[k, half, 0, core], s1_sem.at[k, half],
                       relay_sem.at[k, half], ring_device(half, up, c))
                remote(packed.at[k, half, far, c, 1], relay.at[k, half, 1, core], s1_sem.at[k, half],
                       relay_sem.at[k, half], ring_device(half, down, c))
            other = 1 - core
            here = at(x, y, other)
            remote(packed.at[k, half, up, other, 0], sibling.at[k, half, 0], s1_sem.at[k, half],
                   sibling_sem.at[k, half], here)
            remote(packed.at[k, half, down, other, 1], sibling.at[k, half, 1], s1_sem.at[k, half],
                   sibling_sem.at[k, half], here)
            remote(packed.at[k, half, r, other], sibling.at[k, half, pl.ds(2, 2)], s1_sem.at[k, half],
                   sibling_sem.at[k, half], here)

    def start_directs(k):
        for half in range(2):
            r, _ = ring(half)
            up, down = rem(r + 1, 4), rem(r + 3, 4)
            for c in range(2):
                remote(packed.at[k, half, up, c, 1], direct.at[k, half, 0, core], s1_sem.at[k, half],
                       direct_sem.at[k, half], ring_device(half, up, c))
                remote(packed.at[k, half, down, c, 0], direct.at[k, half, 1, core], s1_sem.at[k, half],
                       direct_sem.at[k, half], ring_device(half, down, c))

    def start_forwards(k):
        for half in range(2):
            r, _ = ring(half)
            up, down = rem(r + 1, 4), rem(r + 3, 4)
            wait(sibling.at[k, half], sibling_sem.at[k, half])
            wait(relay.at[k, half], relay_sem.at[k, half])
            for way, to in ((0, up), (1, down)):
                forward[k, half, way] = (
                    packed[k, half, to, core, way].astype(F32)
                    + sibling[k, half, way].astype(F32)
                    + relay[k, half, way, 0].astype(F32)
                    + relay[k, half, way, 1].astype(F32)
                )
                remote(forward.at[k, half, way], forwarded.at[k, half, way], fw_sem.at[k, half],
                       forwarded_sem.at[k, half], ring_device(half, to, core))

    def start_cross(k):
        for half in range(2):
            r, q = ring(half)
            wait(direct.at[k, half], direct_sem.at[k, half])
            wait(forwarded.at[k, half], forwarded_sem.at[k, half])
            for sub in range(2):
                total = (
                    packed[k, half, r, core, sub].astype(F32)
                    + sibling[k, half, 2 + sub].astype(F32)
                    + forwarded[k, half, sub]
                    + direct[k, half, 1 - sub, 0].astype(F32)
                    + direct[k, half, 1 - sub, 1].astype(F32)
                )
                for to in range(4):
                    part[k, half, to, sub] = total[to]
            up, down, far = rem(q + 1, 4), rem(q + 3, 4), rem(q + 2, 4)
            for way, to in ((0, up), (1, down)):
                remote(part.at[k, half, far, way], cross_relay.at[k, half, way], s2_sem.at[k, half],
                       cross_relay_sem.at[k, half], cross_device(half, to))
            for way, to in ((0, up), (1, down)):
                remote(part.at[k, half, to, 1 - way], cross_direct.at[k, half, way], s2_sem.at[k, half],
                       cross_direct_sem.at[k, half], cross_device(half, to))

    def start_cross_forwards(k):
        for half in range(2):
            _, q = ring(half)
            up, down = rem(q + 1, 4), rem(q + 3, 4)
            wait(cross_relay.at[k, half], cross_relay_sem.at[k, half])
            for way, to in ((0, up), (1, down)):
                cross_forward[k, half, way] = part[k, half, to, way] + cross_relay[k, half, way]
                remote(cross_forward.at[k, half, way], cross_forwarded.at[k, half, way], s2_sem.at[k, half],
                       cross_forwarded_sem.at[k, half], cross_device(half, to))

    lane = lax.broadcasted_iota(jnp.int32, (ROWS, 128), 1)
    heads[HEADS_OWN] = jnp.zeros((ROWS, 128), F32)

    def start_owner(k):
        for half in range(2):
            _, q = ring(half)
            wait(cross_direct.at[k, half], cross_direct_sem.at[k, half])
            wait(cross_forwarded.at[k, half], cross_forwarded_sem.at[k, half])
            for sub in range(2):
                total = part[k, half, q, sub] + cross_forwarded[k, half, sub] + cross_direct[k, half, 1 - sub]
                pair = 2 * half + sub
                heads[2 * pair] = total
                heads[2 * pair + 1] = pltpu.roll(total, 64, 1)

        def fill(t, carry):
            outgoing[k, t] = jnp.where(lane < 64, heads[index[t]], heads[index[OWNERS + t]])
            return carry

        lax.fori_loop(0, OWNERS, fill, 0)
        for i in range(1, OWNERS):
            to = rem(z + i, OWNERS)
            remote(outgoing.at[k, to], arrived.at[k, z], z_send.at[k], z_recv.at[k], {"owner": to})
        arrived[k, z] = outgoing[k, z]

    def wait_owner(k):
        wait(arrived.at[k, pl.ds(0, OWNERS - 1)], z_recv.at[k])

    def start_rows(stage, source, target):
        def send(i, carry):
            s = rem(chip + i, SLOTS_OWN)
            remote(source.at[s], target.at[div(me, 2)], x_send.at[stage], x_recv.at[stage],
                   at(div(s, 4), rem(s, 4), core))
            return carry

        lax.fori_loop(1, SLOTS_OWN, send, 0)
        target[div(me, 2)] = source[chip]

    pack(0)
    pl.semaphore_wait(barrier, len(near) + OWNERS - 1)
    start_relays(0)
    pack(1)
    start_relays(1)
    start_directs(0)
    start_forwards(0)
    loads[4].wait()
    row = logit_row[...]
    mine[...] = jnp.broadcast_to(jnp.concatenate([row, row], axis=1), (8, 128))
    peaks[ctx] = mine[...]
    for i in range(1, 4):
        remote(mine, peaks.at[ctx], l_send, l_recv, {"context": rem(ctx + i, 4)})
    pack(2)
    start_relays(2)
    start_cross(0)
    start_directs(1)
    start_forwards(1)
    start_cross_forwards(0)
    start_directs(2)
    start_forwards(2)

    loads[2].wait()
    named = [table[0, HEADS_OWN * z + i] for i in range(HEADS_OWN)]
    for t in range(OWNERS):
        first, beside, second = jnp.int32(HEADS_OWN), jnp.int32(HEADS_OWN), jnp.int32(HEADS_OWN)
        for i in reversed(range(HEADS_OWN)):
            hit = named[i] == t
            second = jnp.where(hit, beside, second)
            beside = jnp.where(hit, i ^ 1, beside)
            first = jnp.where(hit, i, first)
        index[t] = first
        index[OWNERS + t] = second

    loads[3].wait()
    along = jnp.broadcast_to(targets[...].astype(F32), (HEADS, HEADS))
    head_row = lax.broadcasted_iota(jnp.int32, (HEADS, HEADS), 0)
    head_lane = lax.broadcasted_iota(jnp.int32, (HEADS, HEADS), 1)
    down_column = jnp.sum(jnp.where(head_row == head_lane, along, 0.0), axis=1, keepdims=True)
    earlier = (down_column == along) & (div(head_row, 8) == div(head_lane, 8)) & (head_row < head_lane)
    position = jnp.sum(jnp.where(earlier, 1.0, 0.0), axis=0, keepdims=True)
    slot_row = lax.broadcasted_iota(jnp.int32, (SLOTS_OWN, HEADS), 0)
    slot_lane = lax.broadcasted_iota(jnp.int32, (SLOTS_OWN, HEADS), 1)
    in_slot = (along[0:SLOTS_OWN] == z.astype(F32)) & (
        (div(slot_lane, 8) * 2).astype(F32) + position == slot_row.astype(F32)
    )
    wait(peaks.at[pl.ds(0, 3)], l_recv)
    gamma = jnp.minimum(1.0, LOGIT_CAP / jnp.max(peaks[...], axis=0))
    occupied = jnp.sum(jnp.where(in_slot, 1.0, 0.0), axis=1, keepdims=True) > 0.5
    slot_gamma = jnp.where(
        occupied, jnp.sum(jnp.where(in_slot, gamma[0:1, 0:HEADS], 0.0), axis=1, keepdims=True), 1.0
    )
    rate = jnp.where(occupied, MOMENTUM_RATE, 1.0)
    keep = jnp.where(occupied, WEIGHT_KEEP, 1.0)
    step_size = jnp.where(occupied, 0.04 * math.sqrt(max(QR, QK)), 0.0)
    slot_root = jnp.sqrt(slot_gamma)
    home = lax.broadcasted_iota(jnp.int32, (8, 128), 1) == lax.broadcasted_iota(jnp.int32, (8, 128), 0) + 8 * z
    home_root = jnp.sqrt(jnp.sum(jnp.where(home, gamma, 0.0), axis=1, keepdims=True))
    loads[1].wait()
    for h in range(HEADS_OWN):
        kwt[h] = kwt[h] * home_root[h : h + 1, :]
    stores = [
        pltpu.make_async_copy(mom, momentum_out, store_sem.at[0]),
        pltpu.make_async_copy(kwt, k_out, store_sem.at[1]),
        pltpu.make_async_copy(scales, scale_out, store_sem.at[2]),
    ]
    stores[1].start()
    scale_lane = lax.broadcasted_iota(jnp.int32, (SLOTS_OWN, 128), 1)
    scales[...] = jnp.where(
        scale_lane == 0, keep, jnp.where(scale_lane == 1, step_size, jnp.where(scale_lane == 2, slot_root, slot_gamma))
    )
    stores[2].start()

    start_owner(0)
    start_cross(1)
    start_cross_forwards(1)
    start_cross(2)
    start_owner(1)
    start_cross_forwards(2)
    start_owner(2)
    loads[0].wait()
    wait_owner(0)
    wait_owner(1)
    for s in range(SLOTS_OWN):
        low, high = arrived[0, s // 2], arrived[1, s // 2]
        if s % 2 == 0:
            got = jnp.where(lane < 64, low, pltpu.roll(high, 64, 1))
        else:
            got = jnp.where(lane < 64, pltpu.roll(low, 64, 1), high)
        value = mom[s, :, 0:128] * rate[s : s + 1, :] + got
        mom[s, :, 0:128] = value
        send_a[s] = value.astype(BF16)
    start_rows(0, send_a, rows_a)
    wait_owner(2)
    for s in range(SLOTS_OWN):
        got = arrived[2, s // 2]
        if s % 2 == 1:
            got = pltpu.roll(got, 64, 1)
        value = mom[s, :, 128:192] * rate[s : s + 1, :] + got[:, 0:64]
        mom[s, :, 128:192] = value
        send_b[s] = jnp.concatenate([value[0:24], value[24:48]], axis=1).astype(BF16)
    start_rows(1, send_b, rows_b)
    stores[0].start()

    others = pl.ds(0, SLOTS_OWN - 1)
    wait(rows_a.at[others], x_recv.at[0])
    wait(rows_b.at[others], x_recv.at[1])
    tail = rows_b[...].astype(F32)
    tail = jnp.concatenate([tail[:, :, 0:64], tail[:, :, 64:128]], axis=1).astype(BF16)
    whole = jnp.concatenate([rows_a[...].reshape(QR // 2, 128), tail.reshape(QR // 2, 64)], axis=1)
    gram_mine[...] = lax.dot_general(whole, whole, (((0,), (0,)), ((), ())), preferred_element_type=F32)
    remote(gram_mine, gram_other, g_send, g_recv, at(x, y, 1 - core))
    wait(gram_other, g_recv)
    gram = gram_mine[...] + gram_other[...]
    diagonal = lax.broadcasted_iota(jnp.int32, (QK, QK), 0) == lax.broadcasted_iota(jnp.int32, (QK, QK), 1)
    square_sum = jnp.sum(jnp.sum(jnp.where(diagonal, gram, 0.0), axis=0, keepdims=True), axis=1, keepdims=True)
    scale = 1.0 / (jnp.sqrt(square_sum) + 1e-07)
    gram = gram * scale * scale
    for step in range(ITERS - 1):
        polynomial = (QUINTIC_B * gram + QUINTIC_C * dot_f32(gram, gram)).astype(BF16)
        total = QUINTIC_A * whole.astype(F32) + jnp.dot(whole, polynomial, preferred_element_type=F32)
        if step == 0:
            total = total * scale
        whole = total.astype(BF16)
        factor = polynomial.astype(F32) + jnp.where(diagonal, QUINTIC_A, 0.0)
        gram = dot_f32(factor, dot_f32(gram, factor))
    iterate[...] = whole
    polynomial = (QUINTIC_B * gram + QUINTIC_C * dot_f32(gram, gram)).astype(BF16)

    def finish_group(n, carry):
        group = rem(n + x, 4)
        rows = iterate[pl.ds(pl.multiple_of(group * 192, 192), 192), :]
        total = QUINTIC_A * rows.astype(F32) + jnp.dot(rows, polynomial, preferred_element_type=F32)
        blocks = pl.ds(pl.multiple_of(group * 4, 4), 4)
        result[blocks, 0:ROWS, :] = total[:, 0:128].astype(BF16).reshape(4, ROWS, 128)
        tail = total[:, 128:192].reshape(4, ROWS, 64)
        result[blocks, ROWS:72, :] = jnp.concatenate([tail[:, 0:24], tail[:, 24:48]], axis=2).astype(BF16)

        def send(i, carry):
            j = group * 4 + rem(i + y, 4)
            b = 2 * j + core

            @pl.when(b != me)
            def _():
                remote(result.at[j], back.at[chip], b_send, b_recv, block(b))

            @pl.when(b == me)
            def _():
                pltpu.make_async_copy(result.at[j], back.at[chip], b_recv).start()

            return carry

        lax.fori_loop(0, 4, send, 0)
        return carry

    lax.fori_loop(0, 4, finish_group, 0)
    wait(back, b_recv)

    for k in range(CHUNKS):
        for half in range(2):
            wait(packed.at[k, half, pl.ds(0, 3)], s1_sem.at[k, half])
            wait(forward.at[k, half], fw_sem.at[k, half])
            wait(part.at[k, half, pl.ds(0, 3)], s2_sem.at[k, half])
        wait(outgoing.at[k, pl.ds(0, OWNERS - 1)], z_send.at[k])
    wait(peaks.at[pl.ds(0, 3)], l_send)

    wait(send_a.at[others], x_send.at[0])
    wait(send_b.at[others], x_send.at[1])
    wait(gram_mine, g_send)
    wait(result.at[others], b_send)
    for copy in stores:
        copy.wait()


def finish(
    made_momentum, made_k, made_scales, made_rows, weight,
    momentum_out, weight_out, k_out,
    mom, kwt, scales, rows, wgt, in_sem, row_sem, weight_sem, out_sem, weight_out_sem,
):
    groups = [pl.ds(4 * g, 4) for g in range(4)]
    scale_in = pltpu.make_async_copy(made_scales, scales, in_sem.at[0])
    scale_in.start()
    rows_in = [pltpu.make_async_copy(made_rows.at[g], rows.at[g], row_sem.at[i]) for i, g in enumerate(groups)]
    weight_in = [pltpu.make_async_copy(weight.at[g], wgt.at[g], weight_sem.at[i]) for i, g in enumerate(groups)]
    plain_in = [
        pltpu.make_async_copy(made_momentum, mom, in_sem.at[1]),
        pltpu.make_async_copy(made_k, kwt, in_sem.at[2]),
    ]
    plain_out = [
        pltpu.make_async_copy(mom, momentum_out, out_sem.at[0]),
        pltpu.make_async_copy(kwt, k_out, out_sem.at[1]),
    ]
    weight_back = [
        pltpu.make_async_copy(wgt.at[g], weight_out.at[g], weight_out_sem.at[i]) for i, g in enumerate(groups)
    ]
    for i in range(2):
        rows_in[i].start()
        weight_in[i].start()
    for copy in plain_in:
        copy.start()
    for i in range(2, 4):
        rows_in[i].start()
        weight_in[i].start()
    scale_in.wait()
    for i in range(4):
        if i == 2:
            for arriving, leaving in zip(plain_in, plain_out):
                arriving.wait()
                leaving.start()
        rows_in[i].wait()
        weight_in[i].wait()
        for s in range(4 * i, 4 * i + 4):
            kept, taken = scales[s : s + 1, 0:1], scales[s : s + 1, 1:2]
            root, gamma = scales[s : s + 1, 2:3], scales[s : s + 1, 3:4]
            fresh = rows[s].astype(F32)
            wgt[s, :, 0:128] = (wgt[s, :, 0:128] * kept - taken * fresh[0:ROWS]) * root
            tail = jnp.concatenate([fresh[ROWS:72, 0:64], fresh[ROWS:72, 64:128]], axis=0)
            wgt[s, :, 128:192] = (wgt[s, :, 128:192] * kept - taken * tail) * gamma
        weight_back[i].start()
    for copy in weight_back + plain_out:
        copy.wait()


def body(grad_partials, assignment, momentum, q_weight, k_weight, max_logits):
    turned = jnp.transpose(grad_partials[0], (1, 2, 0))
    hbm = pl.BlockSpec(memory_space=pltpu.HBM)
    vmem = pl.BlockSpec(memory_space=pltpu.VMEM)
    dma = pltpu.SemaphoreType.DMA
    wide = (4, ROWS, 128)
    momentum_like = jax.ShapeDtypeStruct(momentum.shape, F32)
    k_like = jax.ShapeDtypeStruct(k_weight.shape, F32)
    made = pl.pallas_call(
        kernel,
        out_shape=(
            momentum_like,
            k_like,
            jax.ShapeDtypeStruct((SLOTS_OWN, 128), F32),
            jax.ShapeDtypeStruct((SLOTS_OWN, 72, 128), BF16),
        ),
        in_specs=[hbm] * 5,
        out_specs=(hbm,) * 4,
        scratch_shapes=[
            pltpu.VMEM(momentum.shape, F32),
            pltpu.VMEM(k_weight.shape, F32),
            pltpu.VMEM((SLOTS_OWN, 128), F32),
            pltpu.VMEM((CHUNKS, HEADS_OWN, WIDTH, QR), BF16),
            pltpu.VMEM((CHUNKS, 2, 4, 2, 2) + wide, BF16),
            pltpu.VMEM((CHUNKS, 2, 2, 2) + wide, BF16),
            pltpu.VMEM((CHUNKS, 2, 2, 2) + wide, BF16),
            pltpu.VMEM((CHUNKS, 2, 4) + wide, BF16),
            pltpu.VMEM((CHUNKS, 2, 2) + wide, F32),
            pltpu.VMEM((CHUNKS, 2, 2) + wide, F32),
            pltpu.VMEM((CHUNKS, 2, 4, 2, ROWS, 128), F32),
            pltpu.VMEM((CHUNKS, 2, 2, ROWS, 128), F32),
            pltpu.VMEM((CHUNKS, 2, 2, ROWS, 128), F32),
            pltpu.VMEM((CHUNKS, 2, 2, ROWS, 128), F32),
            pltpu.VMEM((CHUNKS, 2, 2, ROWS, 128), F32),
            pltpu.VMEM((HEADS_OWN + 1, ROWS, 128), F32),
            pltpu.VMEM((CHUNKS, OWNERS, ROWS, 128), F32),
            pltpu.VMEM((CHUNKS, OWNERS, ROWS, 128), F32),
            pltpu.SMEM((2 * OWNERS,), jnp.int32),
            pltpu.SMEM((1, HEADS), jnp.int32),
            pltpu.VMEM((1, HEADS), jnp.int32),
            pltpu.VMEM((1, HEADS), F32),
            pltpu.VMEM((8, 128), F32),
            pltpu.VMEM((4, 8, 128), F32),
            pltpu.VMEM((SLOTS_OWN, ROWS, 128), BF16),
            pltpu.VMEM((SLOTS_OWN, 24, 128), BF16),
            pltpu.VMEM((SLOTS_OWN, ROWS, 128), BF16),
            pltpu.VMEM((SLOTS_OWN, 24, 128), BF16),
            pltpu.VMEM((QK, QK), F32),
            pltpu.VMEM((QK, QK), F32),
            pltpu.VMEM((QR // 2, QK), BF16),
            pltpu.VMEM((SLOTS_OWN, 72, 128), BF16),
            dma((CHUNKS,)),
            dma((5,)),
        ]
        + [dma((CHUNKS, 2))] * 10
        + [dma((CHUNKS,)), dma((CHUNKS,)), dma((2,)), dma((2,)), dma, dma, dma, dma, dma, dma, dma((3,))],
        compiler_params=pltpu.CompilerParams(
            collective_id=0, has_side_effects=True, vmem_limit_bytes=56 * 1024 * 1024
        ),
    )(assignment.reshape(1, HEADS), turned, momentum, k_weight, max_logits)
    return pl.pallas_call(
        finish,
        out_shape=(momentum_like, jax.ShapeDtypeStruct(q_weight.shape, F32), k_like),
        in_specs=[hbm] * 5,
        out_specs=(hbm,) * 3,
        scratch_shapes=[
            pltpu.VMEM(momentum.shape, F32),
            pltpu.VMEM(k_weight.shape, F32),
            pltpu.VMEM((SLOTS_OWN, 128), F32),
            pltpu.VMEM((SLOTS_OWN, 72, 128), BF16),
            pltpu.VMEM(q_weight.shape, F32),
            dma((3,)),
            dma((4,)),
            dma((4,)),
            dma((2,)),
            dma((4,)),
        ],
    )(*made, q_weight)


def solution(mesh):
    placed = (
        P(("dp", "context"), None, "owner", None),
        P(),
        P("owner", ("dp", "context"), None),
        P("owner", ("dp", "context"), None),
        P("owner", ("dp", "context"), None),
        P("context", None),
    )
    return jax.shard_map(
        body,
        mesh=mesh,
        in_specs=placed,
        out_specs=(
            P("owner", ("dp", "context"), None),
            P("owner", ("dp", "context"), None),
            P("owner", ("dp", "context"), None),
        ),
        check_vma=False,
    )
```

```python
import functools
import math

import jax
import jax.numpy as jnp
from jax import lax
from jax.experimental import pallas as pl
from jax.experimental.pallas import tpu as pltpu
from jax.sharding import PartitionSpec as P

QR = 1536
QK = 192
ITERS = 2
MOMENTUM_RATE = 0.95
WEIGHT_KEEP = 0.98
LOGIT_CAP = 100.0
QUINTIC_A = 3.4445
QUINTIC_B = -4.775
QUINTIC_C = 2.0315

MESH = pl.DeviceIdType.MESH
BLOCKS = 32
ROWS = QR // BLOCKS
OWNERS = 8
HEADS_OWN = 8
HEADS = 64
SLOTS_OWN = 16
CHUNKS = 3
WIDTH = QK // CHUNKS
F32 = jnp.float32
BF16 = jnp.bfloat16


def rem(a, n):
    return lax.rem(a, jnp.int32(n))


def div(a, n):
    return lax.div(a, jnp.int32(n))


def dot_f32(a, b):
    a_high, b_high = a.astype(BF16), b.astype(BF16)
    a_low, b_low = (a - a_high.astype(F32)).astype(BF16), (b - b_high.astype(F32)).astype(BF16)
    dot = functools.partial(jnp.dot, preferred_element_type=F32)
    return dot(a_high, b_high) + (dot(a_high, b_low) + dot(a_low, b_high))


def kernel(
    assignment, grad, momentum, k_weight, logits,
    momentum_out, k_out, scale_out, back,
    mom, kwt, scales, raw, packed, relay, direct, sibling, forward, forwarded, part, cross_relay, cross_direct, cross_forward,
    cross_forwarded, heads, outgoing, arrived, index, table, targets, logit_row, mine, peaks,
    send_a, send_b, rows_a, rows_b, gram_mine, gram_other, iterate, result,
    load_sem, state_sem, s1_sem, fw_sem, s2_sem, relay_sem, direct_sem, sibling_sem, forwarded_sem,
    cross_relay_sem, cross_direct_sem, cross_forwarded_sem,
    z_send, z_recv, x_send, x_recv, g_send, g_recv, b_send, b_recv, l_send, l_recv, store_sem,
):
    dp, z, ctx = lax.axis_index("dp"), lax.axis_index("owner"), lax.axis_index("context")
    core, y = rem(ctx, 2), rem(dp, 4)
    x = div(ctx, 2) * 2 + div(dp, 4)
    me = dp * 4 + ctx
    chip = x * 4 + y

    def at(x, y, c):
        return {"dp": rem(x, 2) * 4 + y, "context": div(x, 2) * 2 + c}

    def block(b):
        return {"dp": div(b, 4), "context": rem(b, 4)}

    def ring(half):
        return (x, y) if half == 0 else (y, x)

    def ring_device(half, r, c):
        return at(r, y, c) if half == 0 else at(x, r, c)

    def cross_device(half, q):
        return at(x, q, core) if half == 0 else at(q, y, core)

    def remote(src, dst, send, recv, device):
        copy = pltpu.make_async_remote_copy(
            src_ref=src, dst_ref=dst, send_sem=send, recv_sem=recv, device_id=device, device_id_type=MESH
        )
        copy.start()

    def wait(ref, sem):
        pltpu.make_async_copy(ref, ref, sem).wait()

    for k in range(CHUNKS):
        pltpu.make_async_copy(grad.at[:, k * WIDTH : (k + 1) * WIDTH, :], raw.at[k], load_sem.at[k]).start()
    loads = [
        pltpu.make_async_copy(momentum, mom, state_sem.at[0]),
        pltpu.make_async_copy(k_weight, kwt, state_sem.at[1]),
        pltpu.make_async_copy(assignment, table, state_sem.at[2]),
        pltpu.make_async_copy(assignment, targets, state_sem.at[3]),
        pltpu.make_async_copy(logits, logit_row, state_sem.at[4]),
    ]
    for copy in loads:
        copy.start()

    barrier = pltpu.get_barrier_semaphore()

    def greet_z(i, carry):
        pl.semaphore_signal(barrier, inc=1, device_id={"owner": rem(z + i, OWNERS)}, device_id_type=MESH)
        return carry

    beside = 1 - core
    near = [at(x, y, beside)]
    for c in range(2):
        near += [at(rem(x + i, 4), y, c) for i in (1, 2, 3)] + [at(x, rem(y + i, 4), c) for i in (1, 3)]
    for device in near:
        pl.semaphore_signal(barrier, inc=1, device_id=device, device_id_type=MESH)
    lax.fori_loop(1, OWNERS, greet_z, 0)

    row_at = lax.broadcasted_iota(jnp.int32, (384, 384), 0)
    column_at = lax.broadcasted_iota(jnp.int32, (384, 384), 1)
    eye = (row_at == column_at).astype(BF16)

    def pack(k):
        wait(raw.at[k], load_sem.at[k])
        for half in range(2):
            for group in range(4):
                block_in = raw[k, 4 * half : 4 * half + 4, :, 384 * group : 384 * group + 384]
                turned = lax.dot_general(
                    eye, block_in.reshape(4 * WIDTH, 384), (((1,), (1,)), ((), ())), preferred_element_type=F32
                ).astype(BF16)
                for i in range(8):
                    b = 8 * group + i
                    c_to, y_to, x_to = b % 2, (b // 4) % 4, (b // 2) % 2 * 2 + b // 16
                    r_to, q_to = (x_to, y_to) if half == 0 else (y_to, x_to)
                    for sub in range(2):
                        packed[k, half, r_to, c_to, sub, q_to] = turned[
                            ROWS * i : ROWS * i + ROWS, 128 * sub : 128 * sub + 128
                        ]

    def start_relays(k):
        for half in range(2):
            r, _ = ring(half)
            up, down, far = rem(r + 1, 4), rem(r + 3, 4), rem(r + 2, 4)
            for c in range(2):
                remote(packed.at[k, half, far, c, 0], relay.at[k, half, 0, core], s1_sem.at[k, half],
                       relay_sem.at[k, half], ring_device(half, up, c))
                remote(packed.at[k, half, far, c, 1], relay.at[k, half, 1, core], s1_sem.at[k, half],
                       relay_sem.at[k, half], ring_device(half, down, c))
            other = 1 - core
            here = at(x, y, other)
            remote(packed.at[k, half, up, other, 0], sibling.at[k, half, 0], s1_sem.at[k, half],
                   sibling_sem.at[k, half], here)
            remote(packed.at[k, half, down, other, 1], sibling.at[k, half, 1], s1_sem.at[k, half],
                   sibling_sem.at[k, half], here)
            remote(packed.at[k, half, r, other], sibling.at[k, half, pl.ds(2, 2)], s1_sem.at[k, half],
                   sibling_sem.at[k, half], here)

    def start_directs(k):
        for half in range(2):
            r, _ = ring(half)
            up, down = rem(r + 1, 4), rem(r + 3, 4)
            for c in range(2):
                remote(packed.at[k, half, up, c, 1], direct.at[k, half, 0, core], s1_sem.at[k, half],
                       direct_sem.at[k, half], ring_device(half, up, c))
                remote(packed.at[k, half, down, c, 0], direct.at[k, half, 1, core], s1_sem.at[k, half],
                       direct_sem.at[k, half], ring_device(half, down, c))

    def start_forwards(k):
        for half in range(2):
            r, _ = ring(half)
            up, down = rem(r + 1, 4), rem(r + 3, 4)
            wait(sibling.at[k, half], sibling_sem.at[k, half])
            wait(relay.at[k, half], relay_sem.at[k, half])
            for way, to in ((0, up), (1, down)):
                forward[k, half, way] = (
                    packed[k, half, to, core, way].astype(F32)
                    + sibling[k, half, way].astype(F32)
                    + relay[k, half, way, 0].astype(F32)
                    + relay[k, half, way, 1].astype(F32)
                )
                remote(forward.at[k, half, way], forwarded.at[k, half, way], fw_sem.at[k, half],
                       forwarded_sem.at[k, half], ring_device(half, to, core))

    def start_cross(k):
        for half in range(2):
            r, q = ring(half)
            wait(direct.at[k, half], direct_sem.at[k, half])
            wait(forwarded.at[k, half], forwarded_sem.at[k, half])
            for sub in range(2):
                total = (
                    packed[k, half, r, core, sub].astype(F32)
                    + sibling[k, half, 2 + sub].astype(F32)
                    + forwarded[k, half, sub]
                    + direct[k, half, 1 - sub, 0].astype(F32)
                    + direct[k, half, 1 - sub, 1].astype(F32)
                )
                for to in range(4):
                    part[k, half, to, sub] = total[to]
            up, down, far = rem(q + 1, 4), rem(q + 3, 4), rem(q + 2, 4)
            for way, to in ((0, up), (1, down)):
                remote(part.at[k, half, far, way], cross_relay.at[k, half, way], s2_sem.at[k, half],
                       cross_relay_sem.at[k, half], cross_device(half, to))
            for way, to in ((0, up), (1, down)):
                remote(part.at[k, half, to, 1 - way], cross_direct.at[k, half, way], s2_sem.at[k, half],
                       cross_direct_sem.at[k, half], cross_device(half, to))

    def start_cross_forwards(k):
        for half in range(2):
            _, q = ring(half)
            up, down = rem(q + 1, 4), rem(q + 3, 4)
            wait(cross_relay.at[k, half], cross_relay_sem.at[k, half])
            for way, to in ((0, up), (1, down)):
                cross_forward[k, half, way] = part[k, half, to, way] + cross_relay[k, half, way]
                remote(cross_forward.at[k, half, way], cross_forwarded.at[k, half, way], s2_sem.at[k, half],
                       cross_forwarded_sem.at[k, half], cross_device(half, to))

    lane = lax.broadcasted_iota(jnp.int32, (ROWS, 128), 1)
    heads[HEADS_OWN] = jnp.zeros((ROWS, 128), F32)

    def start_owner(k):
        for half in range(2):
            _, q = ring(half)
            wait(cross_direct.at[k, half], cross_direct_sem.at[k, half])
            wait(cross_forwarded.at[k, half], cross_forwarded_sem.at[k, half])
            for sub in range(2):
                total = part[k, half, q, sub] + cross_forwarded[k, half, sub] + cross_direct[k, half, 1 - sub]
                pair = 2 * half + sub
                heads[2 * pair] = total
                heads[2 * pair + 1] = pltpu.roll(total, 64, 1)

        def fill(t, carry):
            outgoing[k, t] = jnp.where(lane < 64, heads[index[t]], heads[index[OWNERS + t]])
            return carry

        lax.fori_loop(0, OWNERS, fill, 0)
        for i in range(1, OWNERS):
            to = rem(z + i, OWNERS)
            remote(outgoing.at[k, to], arrived.at[k, z], z_send.at[k], z_recv.at[k], {"owner": to})
        arrived[k, z] = outgoing[k, z]

    def wait_owner(k):
        wait(arrived.at[k, pl.ds(0, OWNERS - 1)], z_recv.at[k])

    def start_rows(stage, source, target):
        def send(i, carry):
            s = rem(chip + i, SLOTS_OWN)
            remote(source.at[s], target.at[div(me, 2)], x_send.at[stage], x_recv.at[stage],
                   at(div(s, 4), rem(s, 4), core))
            return carry

        lax.fori_loop(1, SLOTS_OWN, send, 0)
        target[div(me, 2)] = source[chip]

    pack(0)
    pl.semaphore_wait(barrier, len(near) + OWNERS - 1)
    start_relays(0)
    pack(1)
    start_relays(1)
    start_directs(0)
    start_forwards(0)
    loads[4].wait()
    row = logit_row[...]
    mine[...] = jnp.broadcast_to(jnp.concatenate([row, row], axis=1), (8, 128))
    peaks[ctx] = mine[...]
    for i in range(1, 4):
        remote(mine, peaks.at[ctx], l_send, l_recv, {"context": rem(ctx + i, 4)})
    pack(2)
    start_relays(2)
    start_cross(0)
    start_directs(1)
    start_forwards(1)
    start_cross_forwards(0)
    start_directs(2)
    start_forwards(2)

    loads[2].wait()
    named = [table[0, HEADS_OWN * z + i] for i in range(HEADS_OWN)]
    for t in range(OWNERS):
        first, beside, second = jnp.int32(HEADS_OWN), jnp.int32(HEADS_OWN), jnp.int32(HEADS_OWN)
        for i in reversed(range(HEADS_OWN)):
            hit = named[i] == t
            second = jnp.where(hit, beside, second)
            beside = jnp.where(hit, i ^ 1, beside)
            first = jnp.where(hit, i, first)
        index[t] = first
        index[OWNERS + t] = second

    loads[3].wait()
    along = jnp.broadcast_to(targets[...].astype(F32), (HEADS, HEADS))
    head_row = lax.broadcasted_iota(jnp.int32, (HEADS, HEADS), 0)
    head_lane = lax.broadcasted_iota(jnp.int32, (HEADS, HEADS), 1)
    down_column = jnp.sum(jnp.where(head_row == head_lane, along, 0.0), axis=1, keepdims=True)
    earlier = (down_column == along) & (div(head_row, 8) == div(head_lane, 8)) & (head_row < head_lane)
    position = jnp.sum(jnp.where(earlier, 1.0, 0.0), axis=0, keepdims=True)
    slot_row = lax.broadcasted_iota(jnp.int32, (SLOTS_OWN, HEADS), 0)
    slot_lane = lax.broadcasted_iota(jnp.int32, (SLOTS_OWN, HEADS), 1)
    in_slot = (along[0:SLOTS_OWN] == z.astype(F32)) & (
        (div(slot_lane, 8) * 2).astype(F32) + position == slot_row.astype(F32)
    )
    wait(peaks.at[pl.ds(0, 3)], l_recv)
    gamma = jnp.minimum(1.0, LOGIT_CAP / jnp.max(peaks[...], axis=0))
    occupied = jnp.sum(jnp.where(in_slot, 1.0, 0.0), axis=1, keepdims=True) > 0.5
    slot_gamma = jnp.where(
        occupied, jnp.sum(jnp.where(in_slot, gamma[0:1, 0:HEADS], 0.0), axis=1, keepdims=True), 1.0
    )
    rate = jnp.where(occupied, MOMENTUM_RATE, 1.0)
    keep = jnp.where(occupied, WEIGHT_KEEP, 1.0)
    step_size = jnp.where(occupied, 0.04 * math.sqrt(max(QR, QK)), 0.0)
    slot_root = jnp.sqrt(slot_gamma)
    home = lax.broadcasted_iota(jnp.int32, (8, 128), 1) == lax.broadcasted_iota(jnp.int32, (8, 128), 0) + 8 * z
    home_root = jnp.sqrt(jnp.sum(jnp.where(home, gamma, 0.0), axis=1, keepdims=True))
    loads[1].wait()
    for h in range(HEADS_OWN):
        kwt[h] = kwt[h] * home_root[h : h + 1, :]
    stores = [
        pltpu.make_async_copy(mom, momentum_out, store_sem.at[0]),
        pltpu.make_async_copy(kwt, k_out, store_sem.at[1]),
        pltpu.make_async_copy(scales, scale_out, store_sem.at[2]),
    ]
    stores[1].start()
    scale_lane = lax.broadcasted_iota(jnp.int32, (SLOTS_OWN, 128), 1)
    scales[...] = jnp.where(
        scale_lane == 0, keep, jnp.where(scale_lane == 1, step_size, jnp.where(scale_lane == 2, slot_root, slot_gamma))
    )
    stores[2].start()

    start_owner(0)
    start_cross(1)
    start_cross_forwards(1)
    start_cross(2)
    start_owner(1)
    start_cross_forwards(2)
    start_owner(2)
    loads[0].wait()
    wait_owner(0)
    wait_owner(1)
    for s in range(SLOTS_OWN):
        low, high = arrived[0, s // 2], arrived[1, s // 2]
        if s % 2 == 0:
            got = jnp.where(lane < 64, low, pltpu.roll(high, 64, 1))
        else:
            got = jnp.where(lane < 64, pltpu.roll(low, 64, 1), high)
        value = mom[s, :, 0:128] * rate[s : s + 1, :] + got
        mom[s, :, 0:128] = value
        send_a[s] = value.astype(BF16)
    start_rows(0, send_a, rows_a)
    wait_owner(2)
    for s in range(SLOTS_OWN):
        got = arrived[2, s // 2]
        if s % 2 == 1:
            got = pltpu.roll(got, 64, 1)
        value = mom[s, :, 128:192] * rate[s : s + 1, :] + got[:, 0:64]
        mom[s, :, 128:192] = value
        send_b[s] = jnp.concatenate([value[0:24], value[24:48]], axis=1).astype(BF16)
    start_rows(1, send_b, rows_b)
    stores[0].start()

    others = pl.ds(0, SLOTS_OWN - 1)
    wait(rows_a.at[others], x_recv.at[0])
    wait(rows_b.at[others], x_recv.at[1])
    tail = rows_b[...].astype(F32)
    tail = jnp.concatenate([tail[:, :, 0:64], tail[:, :, 64:128]], axis=1).astype(BF16)
    whole = jnp.concatenate([rows_a[...].reshape(QR // 2, 128), tail.reshape(QR // 2, 64)], axis=1)
    gram_mine[...] = lax.dot_general(whole, whole, (((0,), (0,)), ((), ())), preferred_element_type=F32)
    remote(gram_mine, gram_other, g_send, g_recv, at(x, y, 1 - core))
    wait(gram_other, g_recv)
    gram = gram_mine[...] + gram_other[...]
    diagonal = lax.broadcasted_iota(jnp.int32, (QK, QK), 0) == lax.broadcasted_iota(jnp.int32, (QK, QK), 1)
    square_sum = jnp.sum(jnp.sum(jnp.where(diagonal, gram, 0.0), axis=0, keepdims=True), axis=1, keepdims=True)
    scale = 1.0 / (jnp.sqrt(square_sum) + 1e-07)
    gram = gram * scale * scale
    for step in range(ITERS - 1):
        polynomial = (QUINTIC_B * gram + QUINTIC_C * dot_f32(gram, gram)).astype(BF16)
        total = QUINTIC_A * whole.astype(F32) + jnp.dot(whole, polynomial, preferred_element_type=F32)
        if step == 0:
            total = total * scale
        whole = total.astype(BF16)
        factor = polynomial.astype(F32) + jnp.where(diagonal, QUINTIC_A, 0.0)
        gram = dot_f32(factor, dot_f32(gram, factor))
    iterate[...] = whole
    polynomial = (QUINTIC_B * gram + QUINTIC_C * dot_f32(gram, gram)).astype(BF16)

    def finish_group(n, carry):
        group = rem(n + x, 4)
        rows = iterate[pl.ds(pl.multiple_of(group * 192, 192), 192), :]
        total = QUINTIC_A * rows.astype(F32) + jnp.dot(rows, polynomial, preferred_element_type=F32)
        blocks = pl.ds(pl.multiple_of(group * 4, 4), 4)
        result[blocks, 0:ROWS, :] = total[:, 0:128].astype(BF16).reshape(4, ROWS, 128)
        tail = total[:, 128:192].reshape(4, ROWS, 64)
        result[blocks, ROWS:72, :] = jnp.concatenate([tail[:, 0:24], tail[:, 24:48]], axis=2).astype(BF16)

        def send(i, carry):
            j = group * 4 + rem(i + y, 4)
            b = 2 * j + core

            @pl.when(b != me)
            def _():
                remote(result.at[j], back.at[chip], b_send, b_recv, block(b))

            @pl.when(b == me)
            def _():
                pltpu.make_async_copy(result.at[j], back.at[chip], b_recv).start()

            return carry

        for i in range(4):
            send(jnp.int32(i), 0)
        return carry

    lax.fori_loop(0, 4, finish_group, 0)
    wait(back, b_recv)

    for k in range(CHUNKS):
        for half in range(2):
            wait(packed.at[k, half, pl.ds(0, 3)], s1_sem.at[k, half])
            wait(forward.at[k, half], fw_sem.at[k, half])
            wait(part.at[k, half, pl.ds(0, 3)], s2_sem.at[k, half])
        wait(outgoing.at[k, pl.ds(0, OWNERS - 1)], z_send.at[k])
    wait(peaks.at[pl.ds(0, 3)], l_send)

    wait(send_a.at[others], x_send.at[0])
    wait(send_b.at[others], x_send.at[1])
    wait(gram_mine, g_send)
    wait(result.at[others], b_send)
    for copy in stores:
        copy.wait()


def finish(
    made_momentum, made_k, made_scales, made_rows, weight,
    momentum_out, weight_out, k_out,
    mom, kwt, scales, rows, wgt, in_sem, row_sem, weight_sem, out_sem, weight_out_sem,
):
    groups = [pl.ds(4 * g, 4) for g in range(4)]
    scale_in = pltpu.make_async_copy(made_scales, scales, in_sem.at[0])
    scale_in.start()
    rows_in = [pltpu.make_async_copy(made_rows.at[g], rows.at[g], row_sem.at[i]) for i, g in enumerate(groups)]
    weight_in = [pltpu.make_async_copy(weight.at[g], wgt.at[g], weight_sem.at[i]) for i, g in enumerate(groups)]
    plain_in = [
        pltpu.make_async_copy(made_momentum, mom, in_sem.at[1]),
        pltpu.make_async_copy(made_k, kwt, in_sem.at[2]),
    ]
    plain_out = [
        pltpu.make_async_copy(mom, momentum_out, out_sem.at[0]),
        pltpu.make_async_copy(kwt, k_out, out_sem.at[1]),
    ]
    weight_back = [
        pltpu.make_async_copy(wgt.at[g], weight_out.at[g], weight_out_sem.at[i]) for i, g in enumerate(groups)
    ]
    for i in range(2):
        rows_in[i].start()
        weight_in[i].start()
    for copy in plain_in:
        copy.start()
    for i in range(2, 4):
        rows_in[i].start()
        weight_in[i].start()
    scale_in.wait()
    for i in range(4):
        if i == 2:
            for arriving, leaving in zip(plain_in, plain_out):
                arriving.wait()
                leaving.start()
        rows_in[i].wait()
        weight_in[i].wait()
        for s in range(4 * i, 4 * i + 4):
            kept, taken = scales[s : s + 1, 0:1], scales[s : s + 1, 1:2]
            root, gamma = scales[s : s + 1, 2:3], scales[s : s + 1, 3:4]
            fresh = rows[s].astype(F32)
            wgt[s, :, 0:128] = (wgt[s, :, 0:128] * kept - taken * fresh[0:ROWS]) * root
            tail = jnp.concatenate([fresh[ROWS:72, 0:64], fresh[ROWS:72, 64:128]], axis=0)
            wgt[s, :, 128:192] = (wgt[s, :, 128:192] * kept - taken * tail) * gamma
        weight_back[i].start()
    for copy in weight_back + plain_out:
        copy.wait()


def body(grad_partials, assignment, momentum, q_weight, k_weight, max_logits):
    turned = jnp.transpose(grad_partials[0], (1, 2, 0))
    hbm = pl.BlockSpec(memory_space=pltpu.HBM)
    vmem = pl.BlockSpec(memory_space=pltpu.VMEM)
    dma = pltpu.SemaphoreType.DMA
    wide = (4, ROWS, 128)
    momentum_like = jax.ShapeDtypeStruct(momentum.shape, F32)
    k_like = jax.ShapeDtypeStruct(k_weight.shape, F32)
    made = pl.pallas_call(
        kernel,
        out_shape=(
            momentum_like,
            k_like,
            jax.ShapeDtypeStruct((SLOTS_OWN, 128), F32),
            jax.ShapeDtypeStruct((SLOTS_OWN, 72, 128), BF16),
        ),
        in_specs=[hbm] * 5,
        out_specs=(hbm,) * 4,
        scratch_shapes=[
            pltpu.VMEM(momentum.shape, F32),
            pltpu.VMEM(k_weight.shape, F32),
            pltpu.VMEM((SLOTS_OWN, 128), F32),
            pltpu.VMEM((CHUNKS, HEADS_OWN, WIDTH, QR), BF16),
            pltpu.VMEM((CHUNKS, 2, 4, 2, 2) + wide, BF16),
            pltpu.VMEM((CHUNKS, 2, 2, 2) + wide, BF16),
            pltpu.VMEM((CHUNKS, 2, 2, 2) + wide, BF16),
            pltpu.VMEM((CHUNKS, 2, 4) + wide, BF16),
            pltpu.VMEM((CHUNKS, 2, 2) + wide, F32),
            pltpu.VMEM((CHUNKS, 2, 2) + wide, F32),
            pltpu.VMEM((CHUNKS, 2, 4, 2, ROWS, 128), F32),
            pltpu.VMEM((CHUNKS, 2, 2, ROWS, 128), F32),
            pltpu.VMEM((CHUNKS, 2, 2, ROWS, 128), F32),
            pltpu.VMEM((CHUNKS, 2, 2, ROWS, 128), F32),
            pltpu.VMEM((CHUNKS, 2, 2, ROWS, 128), F32),
            pltpu.VMEM((HEADS_OWN + 1, ROWS, 128), F32),
            pltpu.VMEM((CHUNKS, OWNERS, ROWS, 128), F32),
            pltpu.VMEM((CHUNKS, OWNERS, ROWS, 128), F32),
            pltpu.SMEM((2 * OWNERS,), jnp.int32),
            pltpu.SMEM((1, HEADS), jnp.int32),
            pltpu.VMEM((1, HEADS), jnp.int32),
            pltpu.VMEM((1, HEADS), F32),
            pltpu.VMEM((8, 128), F32),
            pltpu.VMEM((4, 8, 128), F32),
            pltpu.VMEM((SLOTS_OWN, ROWS, 128), BF16),
            pltpu.VMEM((SLOTS_OWN, 24, 128), BF16),
            pltpu.VMEM((SLOTS_OWN, ROWS, 128), BF16),
            pltpu.VMEM((SLOTS_OWN, 24, 128), BF16),
            pltpu.VMEM((QK, QK), F32),
            pltpu.VMEM((QK, QK), F32),
            pltpu.VMEM((QR // 2, QK), BF16),
            pltpu.VMEM((SLOTS_OWN, 72, 128), BF16),
            dma((CHUNKS,)),
            dma((5,)),
        ]
        + [dma((CHUNKS, 2))] * 10
        + [dma((CHUNKS,)), dma((CHUNKS,)), dma((2,)), dma((2,)), dma, dma, dma, dma, dma, dma, dma((3,))],
        compiler_params=pltpu.CompilerParams(
            collective_id=0, has_side_effects=True, vmem_limit_bytes=56 * 1024 * 1024
        ),
    )(assignment.reshape(1, HEADS), turned, momentum, k_weight, max_logits)
    return pl.pallas_call(
        finish,
        out_shape=(momentum_like, jax.ShapeDtypeStruct(q_weight.shape, F32), k_like),
        in_specs=[hbm] * 5,
        out_specs=(hbm,) * 3,
        scratch_shapes=[
            pltpu.VMEM(momentum.shape, F32),
            pltpu.VMEM(k_weight.shape, F32),
            pltpu.VMEM((SLOTS_OWN, 128), F32),
            pltpu.VMEM((SLOTS_OWN, 72, 128), BF16),
            pltpu.VMEM(q_weight.shape, F32),
            dma((3,)),
            dma((4,)),
            dma((4,)),
            dma((2,)),
            dma((4,)),
        ],
    )(*made, q_weight)


def solution(mesh):
    placed = (
        P(("dp", "context"), None, "owner", None),
        P(),
        P("owner", ("dp", "context"), None),
        P("owner", ("dp", "context"), None),
        P("owner", ("dp", "context"), None),
        P("context", None),
    )
    return jax.shard_map(
        body,
        mesh=mesh,
        in_specs=placed,
        out_specs=(
            P("owner", ("dp", "context"), None),
            P("owner", ("dp", "context"), None),
            P("owner", ("dp", "context"), None),
        ),
        check_vma=False,
    )
```
